32 devices in a mesh: gx: 2 (over x), gz: 4 (over y, core), ta: 4 (over z).
Axes of the slice: x: 2, y: 2, z: 4, core: 2. Of those that a mesh axis runs over, the one named last changes fastest.
Arguments:
- velocity: bfloat16 [3, 32, 64, 4096], P(None, 'ta', 'gx', 'gz'), may hold values from -6 to 6
- offsets: int32 [7], replicated, may hold values from 0 to 16, as said below
- owner: int32 [7], replicated, may hold values from 0 to 7, as said below
Outputs:
- cross_spectra: float32 [4, 2, 7, 64, 4096], P(None, None, None, 'gx', ('gz', 'ta'))
The draws below stay inside these ranges and needn't reach their ends.
Inputs may be any that keep to these rules, and one draw needn't show every extreme that they name: `offsets`: each segment of 16 snapshots lies inside the window. owner o names the block of streamwise index o // 4 and spanwise index o mod 4.
All inputs are finite; a program needn't handle non-finite values.
Results may differ from the reference program's by a relative error of at most 0.0062.
Values may be sent and summed in bfloat16 or wider, within the bound.
No kernel may reach another device: no remote copies, remote signals or barrier semaphores. Data moves between devices by JAX's collectives and lax.ppermute only.
A program may use at most 64 MiB of HBM per device.

```python
import math
import jax
import jax.numpy as jnp
from jax import lax

CX = 32
CZ = 1024
SEG = 16
NSEG = 7
F = 7
NT = 32
NX = 64
NZ = 4096
BLOCKS_X = 2
BLOCKS_Z = 4


def draw_offsets(key, part):
    latest = NT - SEG
    sampled_values = jax.random.randint(key, (NSEG,), 0, latest + 1)
    placing = jax.random.permutation(jax.random.fold_in(key, 7), NSEG)
    sampled_values = sampled_values.at[placing[0]].set(0)
    sampled_values = sampled_values.at[placing[1]].set(latest)
    return sampled_values.astype(jnp.int32)


def draw_owner(key, part):
    latest = BLOCKS_X * BLOCKS_Z - 1
    sampled_values = jax.random.randint(key, (NSEG,), 0, latest + 1)
    placing = jax.random.permutation(jax.random.fold_in(key, 11), NSEG)
    sampled_values = sampled_values.at[placing[0]].set(0)
    sampled_values = sampled_values.at[placing[1]].set(latest)
    return sampled_values.astype(jnp.int32)


def block_scale(rng, extent, split, smallest, high):
    level = 1.0
    for dim, blocks in split:
        steps = jax.random.uniform(jax.random.fold_in(jax.random.fold_in(rng, 6), dim), (blocks,), jnp.float32, smallest / len(split), high / len(split))
        level = level * jnp.repeat(jnp.exp(steps), extent[dim] // blocks).reshape((-1,) + (1,) * (len(extent) - 1 - dim))
    return level


def centred(stream_key, dims, scale, most, cuts=(), held_as=jnp.bfloat16):
    result = scale * jax.random.normal(stream_key, dims, jnp.float32)
    if cuts:
        result = result * block_scale(stream_key, dims, cuts, -0.22, 0.18)
    return jnp.clip(result, -most, most).astype(held_as)


def setup_inputs(seed: int = 0) -> dict:
    key_of = jax.random.split(jax.random.key(seed), 4)
    velocity = centred(key_of[0], (3, NT, NX, NZ), 1.0, 6.0, ((1, 4), (2, 2), (3, 4)))
    offsets = draw_offsets(jax.random.fold_in(key_of[3], 71), 0)
    owner = draw_owner(jax.random.fold_in(key_of[3], 71), 0)
    return {"velocity": velocity, "offsets": offsets, "owner": owner}


def wrapped_gradient(field, which_axis):
    ahead_one = jnp.roll(field, -1, which_axis)
    behind_one = jnp.roll(field, 1, which_axis)
    ahead_two = jnp.roll(field, -2, which_axis)
    behind_two = jnp.roll(field, 2, which_axis)
    return (8.0 * (ahead_one - behind_one) - (ahead_two - behind_two)) / 12.0


def dft_table(offsets, step_count_total):
    sample_times = jnp.arange(step_count_total, dtype=jnp.int32)
    temporal_delay = sample_times[None, :] - offsets[:, None].astype(jnp.int32)
    inside = (temporal_delay >= 0) & (temporal_delay < SEG)
    window = 0.5 - 0.5 * jnp.cos((2.0 * math.pi / SEG) * temporal_delay.astype(jnp.float32))
    frequency = jnp.arange(1, F + 1, dtype=jnp.int32)
    turns = (frequency[None, :, None] * temporal_delay[:, None, :]) % SEG
    phase_angle = (2.0 * math.pi / SEG) * turns.astype(jnp.float32)
    weight = jnp.where(inside, window, jnp.float32(0.0))[:, None, :]
    rows = jnp.stack([weight * jnp.cos(phase_angle), -weight * jnp.sin(phase_angle)], axis=1)
    return rows.reshape(offsets.shape[0] * 2 * F, step_count_total).astype(jnp.bfloat16)


def reference(velocity, offsets, owner):
    streamwise = velocity[0].astype(jnp.float32)
    spanwise = velocity[2].astype(jnp.float32)
    vorticity = (wrapped_gradient(streamwise, 2) - wrapped_gradient(spanwise, 1)).astype(jnp.bfloat16)
    fields = jnp.concatenate([velocity, vorticity[None]], axis=0)
    flat_fields = fields.reshape(4, NT, NX * NZ)
    window_rows = dft_table(jnp.zeros((1,), jnp.int32), SEG)
    zero_index = jnp.zeros((), jnp.int32)
    cospectrum = jnp.zeros((4, F, NX, NZ), jnp.float32)
    quadrature_spectrum = jnp.zeros((4, F, NX, NZ), jnp.float32)
    for segment in range(NSEG):
        window_piece = lax.dynamic_slice_in_dim(flat_fields, offsets[segment].astype(jnp.int32), SEG, 1)
        spectrum = jnp.stack([jnp.dot(window_rows, window_piece[quantity], preferred_element_type=jnp.float32) for quantity in range(4)])
        spectrum = spectrum.reshape(4, 2, F, NX, NZ)
        start_x = (owner[segment] // BLOCKS_Z).astype(jnp.int32) * CX
        start_z = (owner[segment] % BLOCKS_Z).astype(jnp.int32) * CZ
        block_data = lax.dynamic_slice(spectrum, (zero_index, zero_index, zero_index, start_x, start_z), (4, 2, F, CX, CZ))
        remote = jnp.tile(block_data, (1, 1, 1, BLOCKS_X, BLOCKS_Z))
        cospectrum = cospectrum + (remote[:, 0] * spectrum[:, 0] + remote[:, 1] * spectrum[:, 1])
        quadrature_spectrum = quadrature_spectrum + (remote[:, 0] * spectrum[:, 1] - remote[:, 1] * spectrum[:, 0])
    scaling = 8.0 / (3.0 * SEG * NSEG)
    return jnp.stack([cospectrum, quadrature_spectrum], axis=1) * scaling
```

```python
import functools
import math

import jax
import jax.numpy as jnp
from jax import lax
from jax.experimental import pallas as pl
from jax.experimental.pallas import tpu as pltpu
from jax.sharding import PartitionSpec as P

SEG = 16
NSEG = 7
F = 7
ROWS = 16
LANES = 128


def partner(index, step, count):
    if count & (count - 1) == 0:
        return index ^ step
    return (step - index) % count


def trade(x, axis, step):
    count = lax.axis_size(axis)
    return lax.ppermute(x, axis, [(i, partner(i, step, count)) for i in range(count)])


def dft_rows(offsets, nt):
    lag = jnp.arange(nt, dtype=jnp.int32)[None, :] - offsets[:, None]
    inside = (lag >= 0) & (lag < SEG)
    window = 0.5 - 0.5 * jnp.cos((2.0 * math.pi / SEG) * lag.astype(jnp.float32))
    frequency = jnp.arange(1, 9, dtype=jnp.int32)
    turns = (frequency[None, :, None] * lag[:, None, :]) % SEG
    angle = (2.0 * math.pi / SEG) * turns.astype(jnp.float32)
    keep = inside[:, None, :] & (frequency <= F)[None, :, None]
    weight = jnp.where(keep, window[:, None, :], jnp.float32(0.0))
    rows = jnp.stack([weight * jnp.cos(angle), -weight * jnp.sin(angle)], axis=1)
    return rows.reshape(offsets.shape[0] * ROWS, nt).astype(jnp.bfloat16)


def split_slabs(velocity, quantity, place, steps):
    _, tl, xb, zb = velocity.shape
    count = len(steps) + 1
    cs = zb // count

    def body(place_ref, vel, *rest):
        outs, sem = rest[:-1], rest[-1]
        copies = []
        for n, step in enumerate(steps):
            to = partner(place_ref[0], step, count)
            copies.append(
                pltpu.make_async_copy(
                    vel.at[quantity, :, :, pl.ds(pl.multiple_of(to * cs, LANES), cs)], outs[n], sem.at[n]
                )
            )
        for copy in copies:
            copy.start()
        for copy in copies:
            copy.wait()

    return pl.pallas_call(
        body,
        grid_spec=pltpu.PrefetchScalarGridSpec(
            num_scalar_prefetch=1,
            grid=(1,),
            in_specs=[pl.BlockSpec(memory_space=pl.ANY)],
            out_specs=[pl.BlockSpec(memory_space=pl.ANY) for _ in steps],
            scratch_shapes=[pltpu.SemaphoreType.DMA((len(steps),))],
        ),
        out_shape=[jax.ShapeDtypeStruct((tl, xb, cs), velocity.dtype) for _ in steps],
        name="split_slabs",
    )(place, velocity)


def rows_first(velocity, quantity, parts, place, edges):
    tl, xb, cs = parts[0].shape
    count = len(parts) + 1
    nt = tl * count
    rb = 16
    tiles = cs // LANES

    def body(place_ref, own, *rest):
        others = rest[: count - 1]
        out = rest[count - 1]
        wide = rest[-1]
        for m in range(count):
            x = own[0] if m == 0 else others[m - 1][...]
            t_block = partner(place_ref[0], m, count)
            x = x.astype(jnp.float32)
            for c in range(tiles):
                wide[c, pl.ds(pl.multiple_of(t_block * (tl * rb), 8), tl * rb), :] = x[
                    :, :, c * LANES : (c + 1) * LANES
                ].reshape(tl * rb, LANES)
        for r in range(rb):
            for c in range(tiles):
                series = wide[c, pl.ds(r, nt, stride=rb), :]
                out[r, :, c * LANES : (c + 1) * LANES] = series.astype(jnp.bfloat16)
        if edges:
            edge_out = rest[count]
            which = lax.broadcasted_iota(jnp.int32, (8, cs), 0)
            column = lax.broadcasted_iota(jnp.int32, (8, cs), 1)
            wanted = jnp.where(which < 2, which, cs - 4 + which)
            pick = jnp.where((wanted == column) & (which < 4), 1.0, 0.0).astype(jnp.bfloat16)
            picked = lax.dot_general(
                pick,
                out[...].reshape(rb * nt, cs),
                (((1,), (1,)), ((), ())),
                preferred_element_type=jnp.float32,
            )
            edge_out[...] = picked.astype(jnp.bfloat16)

    out_shape = [jax.ShapeDtypeStruct((xb, nt, cs), velocity.dtype)]
    out_specs = [pl.BlockSpec((rb, nt, cs), lambda i, p: (i, 0, 0))]
    if edges:
        out_shape.append(jax.ShapeDtypeStruct((8, xb * nt), velocity.dtype))
        out_specs.append(pl.BlockSpec((8, rb * nt), lambda i, p: (0, i)))
    return pl.pallas_call(
        body,
        grid_spec=pltpu.PrefetchScalarGridSpec(
            num_scalar_prefetch=1,
            grid=(xb // rb,),
            in_specs=[pl.BlockSpec((1, tl, rb, cs), lambda i, p: (quantity, 0, i, p[0]))]
            + [pl.BlockSpec((tl, rb, cs), lambda i, p: (0, i, 0)) for _ in parts],
            out_specs=out_specs,
            scratch_shapes=[pltpu.VMEM((tiles, nt * rb, LANES), jnp.float32)],
        ),
        out_shape=out_shape,
        name="rows_first",
    )(place, velocity, *parts)


def vorticity(stream, span, edge_before, edge_after, span_before, span_after):
    xb, nt, cs = stream.shape

    def body(u, w, left, right, before, after, out, wide, slope):
        column = lax.broadcasted_iota(jnp.int32, (cs, cs), 1)
        ahead = lax.broadcasted_iota(jnp.int32, (cs, cs), 0) - column
        taps = (
            jnp.where(ahead == 1, 8.0, 0.0)
            - jnp.where(ahead == -1, 8.0, 0.0)
            - jnp.where(ahead == 2, 1.0, 0.0)
            + jnp.where(ahead == -2, 1.0, 0.0)
        ).astype(jnp.bfloat16)
        which = lax.broadcasted_iota(jnp.int32, (8, cs), 0)
        column = lax.broadcasted_iota(jnp.int32, (8, cs), 1)
        behind = column - (which - 4)
        left_taps = jnp.where(
            (which == 2) | (which == 3),
            jnp.where(behind == 2, 1.0, 0.0) - jnp.where(behind == 1, 8.0, 0.0),
            0.0,
        )
        beyond = cs + which - column
        right_taps = jnp.where(
            which < 2, jnp.where(beyond == 1, 8.0, 0.0) - jnp.where(beyond == 2, 1.0, 0.0), 0.0
        )
        side_taps = jnp.concatenate([left_taps, right_taps], axis=0).astype(jnp.bfloat16)
        sides = jnp.concatenate([left[...].astype(jnp.float32), right[...].astype(jnp.float32)], axis=0)
        sides = sides.T.astype(jnp.bfloat16)
        slope[...] = jnp.dot(
            u[...].reshape(xb * nt, cs), taps, preferred_element_type=jnp.float32
        ) + jnp.dot(sides, side_taps, preferred_element_type=jnp.float32)
        wide[0:2] = before[...].astype(jnp.float32)
        wide[2 : 2 + xb] = w[...].astype(jnp.float32)
        wide[2 + xb : 4 + xb] = after[...].astype(jnp.float32)

        def row(r, carry):
            across = 8.0 * (wide[r + 3] - wide[r + 1]) - (wide[r + 4] - wide[r])
            along = slope[pl.ds(pl.multiple_of(r * nt, nt), nt), :]
            out[r] = ((along - across) / 12.0).astype(jnp.bfloat16)
            return carry

        lax.fori_loop(0, xb, row, 0)

    return pl.pallas_call(
        body,
        out_shape=jax.ShapeDtypeStruct((xb, nt, cs), stream.dtype),
        scratch_shapes=[
            pltpu.VMEM((xb + 4, nt, cs), jnp.float32),
            pltpu.VMEM((xb * nt, cs), jnp.float32),
        ],
        name="vorticity",
    )(stream, span, edge_before, edge_after, span_before, span_after)


def cross(series, rows, owner):
    blocks, rc, nt, cs = series.shape
    scaling = 8.0 / (3.0 * SEG * NSEG)

    def body(owner_ref, x, table, out, spec, ref_spec):
        def one_row(r, carry):
            for b in range(blocks):
                spec[b] = jnp.dot(table[...], x[b, r], preferred_element_type=jnp.float32)
            for s in range(NSEG):
                ref_spec[s * ROWS : (s + 1) * ROWS, :] = spec[owner_ref[s], s * ROWS : (s + 1) * ROWS, :]
            for b in range(blocks):
                co = jnp.zeros((8, cs), jnp.float32)
                quad = jnp.zeros((8, cs), jnp.float32)
                for s in range(NSEG):
                    at = s * ROWS
                    rc_, rs_ = ref_spec[at : at + 8, :], ref_spec[at + 8 : at + 16, :]
                    qc, qs = spec[b, at : at + 8, :], spec[b, at + 8 : at + 16, :]
                    co = co + (rc_ * qc + rs_ * qs)
                    quad = quad + (rc_ * qs - rs_ * qc)
                both = jnp.concatenate([co, quad], axis=0) * scaling
                out[b, r] = both.astype(jnp.bfloat16)
            return carry

        lax.fori_loop(0, rc, one_row, 0)

    return pl.pallas_call(
        body,
        grid_spec=pltpu.PrefetchScalarGridSpec(
            num_scalar_prefetch=1,
            grid=(1,),
            in_specs=[
                pl.BlockSpec((blocks, rc, nt, cs), lambda i, o: (0, 0, 0, 0)),
                pl.BlockSpec((NSEG * ROWS, nt), lambda i, o: (0, 0)),
            ],
            out_specs=pl.BlockSpec((blocks, rc, ROWS, cs), lambda i, o: (0, 0, 0, 0)),
            scratch_shapes=[
                pltpu.VMEM((blocks, NSEG * ROWS, cs), jnp.float32),
                pltpu.VMEM((NSEG * ROWS, cs), jnp.float32),
            ],
        ),
        out_shape=jax.ShapeDtypeStruct((blocks, rc, ROWS, cs), jnp.bfloat16),
        name="cross",
    )(owner, series, rows)


def assemble(pieces):
    xb, _, cs = pieces[0].shape
    tiles = cs // LANES
    quantities = len(pieces)

    def body(*refs):
        ins, out, wide = refs[:quantities], refs[quantities], refs[quantities + 1]
        for q in range(quantities):
            @pl.when(pl.program_id(0) == q)
            def _():
                x = ins[q][...].astype(jnp.float32)
                for c in range(tiles):
                    wide[c] = x[:, :, c * LANES : (c + 1) * LANES].reshape(xb * ROWS, LANES)
        for c in range(tiles):
            for part in range(2):
                for k in range(F):
                    out[0, part, k, :, c * LANES : (c + 1) * LANES] = wide[
                        c, pl.ds(part * 8 + k, xb, stride=ROWS), :
                    ]

    return pl.pallas_call(
        body,
        grid=(quantities,),
        in_specs=[pl.BlockSpec((xb, ROWS, cs), lambda q: (0, 0, 0)) for _ in pieces],
        out_specs=pl.BlockSpec((1, 2, F, xb, cs), lambda q: (q, 0, 0, 0, 0)),
        scratch_shapes=[pltpu.VMEM((tiles, xb * ROWS, LANES), jnp.float32)],
        out_shape=jax.ShapeDtypeStruct((quantities, 2, F, xb, cs), jnp.float32),
        name="assemble",
    )(*pieces)


def shards(velocity, offsets, owner):
    _, tl, xb, zb = velocity.shape
    times = lax.axis_size("ta")
    groups = lax.axis_size("gx") * lax.axis_size("gz")
    cs = zb // times
    rc = xb // groups
    nt = tl * times
    steps = list(range(1, times))
    place = lax.axis_index("ta").astype(jnp.int32).reshape(1)

    def gathered(quantity, edges):
        pieces = split_slabs(velocity, quantity, place, steps)
        arrived = [trade(piece, "ta", step) for piece, step in zip(pieces, steps)]
        return rows_first(velocity, quantity, arrived, place, edges)

    def ring(axis):
        size = lax.axis_size(axis)
        up = [(i, (i + 1) % size) for i in range(size)]
        return up, [(j, i) for i, j in up]

    stream, edge = gathered(0, True)
    (span,) = gathered(2, False)
    (wall,) = gathered(1, False)
    up, down = ring(("gz", "ta"))
    edge_before = lax.ppermute(edge, ("gz", "ta"), up)
    edge_after = lax.ppermute(edge, ("gz", "ta"), down)
    up, down = ring("gx")
    span_before = lax.ppermute(span[xb - 2 :], "gx", up)
    span_after = lax.ppermute(span[:2], "gx", down)
    spin = vorticity(stream, span, edge_before, edge_after, span_before, span_after)

    table = dft_rows(offsets, nt)
    results = []
    for field in (stream, span, wall, spin):
        series = lax.all_to_all(
            field.reshape(groups, rc, nt, cs), ("gx", "gz"), split_axis=0, concat_axis=0, tiled=True
        )
        spectra = cross(series, table, owner)
        back = lax.all_to_all(spectra, ("gx", "gz"), split_axis=0, concat_axis=0, tiled=True)
        results.append(back.reshape(xb, ROWS, cs))
    return assemble([results[0], results[2], results[1], results[3]])


def solution(mesh):
    in_specs = (P(None, "ta", "gx", "gz"), P(), P())
    out_specs = P(None, None, None, "gx", ("gz", "ta"))
    return jax.shard_map(shards, mesh=mesh, in_specs=in_specs, out_specs=out_specs, check_vma=False)
```

```python
import math

import jax
import jax.numpy as jnp
import numpy as np
from jax import lax
from jax.experimental import pallas as pl
from jax.experimental.pallas import tpu as pltpu
from jax.sharding import PartitionSpec as P

SEG = 16
NSEG = 7
F = 7
ROWS = 16
LANES = 128


class Plan:
    def __init__(self, velocity):
        _, self.tl, self.xb, self.zb = velocity.shape
        self.gx, self.gz, self.ta = (lax.axis_size(a) for a in ("gx", "gz", "ta"))
        self.blocks = self.gx * self.gz
        self.nt = self.tl * self.ta
        self.cs = self.zb // self.ta
        self.cc = self.cs // self.blocks
        self.groups = LANES // self.cc
        self.rg = self.xb // self.groups
        self.chunks = self.zb // self.cc
        assert self.groups * self.rg == self.xb and self.xb * 4 == LANES and self.cc >= 2
        self.fast = self.rg == 8 and self.tl == 8 and self.cs % LANES == 0


def dft_rows(offsets, times):
    lag = times[None, :] - offsets[:, None]
    inside = (lag >= 0) & (lag < SEG)
    window = 0.5 - 0.5 * jnp.cos((2.0 * math.pi / SEG) * lag.astype(jnp.float32))
    frequency = jnp.arange(1, 9, dtype=jnp.int32)
    turns = (frequency[None, :, None] * lag[:, None, :]) % SEG
    angle = (2.0 * math.pi / SEG) * turns.astype(jnp.float32)
    keep = inside[:, None, :] & (frequency <= F)[None, :, None]
    weight = jnp.where(keep, window[:, None, :], jnp.float32(0.0))
    rows = jnp.stack([weight * jnp.cos(angle), -weight * jnp.sin(angle)], axis=1)
    return rows.reshape(offsets.shape[0] * ROWS, times.shape[0]).astype(jnp.bfloat16)


def exchange_groups(arrays, width):
    arrays = list(arrays)
    lane = lax.broadcasted_iota(jnp.int32, arrays[0].shape, 1)
    step = 1
    while step < len(arrays):
        odd = (lane // (width * step)) % 2 == 1
        for i in range(len(arrays)):
            if i & step == 0:
                a, b = arrays[i], arrays[i + step]
                arrays[i] = jnp.where(odd, pltpu.roll(b, width * step, 1), a)
                arrays[i + step] = jnp.where(odd, b, pltpu.roll(a, LANES - width * step, 1))
        step *= 2
    return arrays


def pack(plan, velocity, quantity, edges):
    p = plan
    shape = (p.blocks, p.ta, p.rg + (1 if edges else 0), p.tl, LANES)
    if not p.fast:
        x = velocity[quantity].reshape(p.tl, p.groups, p.rg, p.ta, p.blocks, p.cc)
        out = x.transpose(4, 3, 2, 0, 1, 5).reshape(p.blocks, p.ta, p.rg, p.tl, LANES)
        if edges:
            x = velocity[quantity].reshape(p.tl, p.xb, p.chunks, p.cc)
            before = jnp.roll(x[..., p.cc - 2 :], 1, axis=2)
            after = jnp.roll(x[..., :2], -1, axis=2)
            side = jnp.concatenate([before, after], axis=3).transpose(2, 0, 1, 3)
            side = side.reshape(p.ta, p.blocks, 1, p.tl, LANES).swapaxes(0, 1)
            out = jnp.concatenate([out, side], axis=2)
        return out
    tiles = p.zb // LANES
    per_slab = p.cs // LANES

    def body(x, out, wide):
        def one_tile(i, carry):
            at = pl.multiple_of(i * LANES, LANES)
            for t in range(p.tl):
                rows = x[0, t, :, pl.ds(at, LANES)].astype(jnp.float32)
                mine = exchange_groups([rows[g * p.rg : (g + 1) * p.rg] for g in range(p.groups)], p.cc)
                for g in range(p.groups):
                    wide[i * p.groups + g, t * p.rg : (t + 1) * p.rg, :] = mine[g]
            for g in range(p.groups):
                for r in range(p.rg):
                    series = wide[i * p.groups + g, pl.ds(r, p.tl, stride=p.rg), :]
                    out[(i % per_slab) * p.groups + g, i // per_slab, r] = series.astype(jnp.bfloat16)
            return carry

        lax.fori_loop(0, tiles, one_tile, 0)
        if edges:
            lane = lax.broadcasted_iota(jnp.int32, (p.tl, LANES), 1)
            slot = lane % p.cc
            side = slot % 4

            def one_chunk(c, carry):
                before = lax.rem(c + p.chunks - 1, p.chunks)
                after = lax.rem(c + 1, p.chunks)
                acc = jnp.zeros((p.tl, LANES), jnp.float32)
                for r in range(p.rg):
                    left = wide[before, pl.ds(r, p.tl, stride=p.rg), :]
                    right = wide[after, pl.ds(r, p.tl, stride=p.rg), :]
                    left = pltpu.roll(left, (4 * r + 2 - p.cc) % LANES, 1)
                    right = pltpu.roll(right, 4 * r + 2, 1)
                    acc = jnp.where(slot // 4 == r, jnp.where(side < 2, left, right), acc)
                out[c % p.blocks, c // p.blocks, p.rg] = acc.astype(jnp.bfloat16)
                return carry

            lax.fori_loop(0, p.chunks, one_chunk, 0)

    return pl.pallas_call(
        body,
        grid=(1,),
        in_specs=[pl.BlockSpec((1, p.tl, p.xb, p.zb), lambda i: (quantity, 0, 0, 0))],
        out_specs=pl.BlockSpec(shape, lambda i: (0,) * 5),
        out_shape=jax.ShapeDtypeStruct(shape, velocity.dtype),
        scratch_shapes=[pltpu.VMEM((p.chunks, p.tl * p.rg, LANES), jnp.float32)],
        name="pack",
    )(velocity)


def slope_taps(plan):
    p = plan
    tap = {1: 8.0, -1: -8.0, 2: -1.0, -2: 1.0}
    inner = np.zeros((LANES, LANES), np.float32)
    outer = np.zeros((LANES, p.rg, LANES), np.float32)
    for g in range(p.groups):
        for c in range(p.cc):
            to = g * p.cc + c
            for ahead, weight in tap.items():
                at = c + ahead
                if 0 <= at < p.cc:
                    inner[g * p.cc + at, to] = weight
                else:
                    side = at + 2 if at < 0 else at - p.cc + 2
                    for r in range(p.rg):
                        outer[(g * p.rg + r) * 4 + side, r, to] = weight
    return jnp.asarray(inner, jnp.bfloat16), jnp.asarray(outer.reshape(LANES, -1), jnp.bfloat16)


def series_of(ref, b, r, parts):
    x = [ref[b, m, r].astype(jnp.float32) for m in range(parts)]
    return jnp.concatenate(x, axis=0)


def vorticity(plan, stream, span, chunk):
    p = plan
    inner, outer = slope_taps(p)

    def body(chunk_ref, u, w, inner_ref, outer_ref, out, sides, slope):
        first = (chunk_ref[0] == 0).astype(jnp.int32)
        last = (chunk_ref[0] == p.chunks - 1).astype(jnp.int32)
        lane = lax.broadcasted_iota(jnp.int32, (p.nt, LANES), 1)
        for a in range(p.gx):
            for z in range(p.gz):
                before = a * p.gz + lax.rem(z + p.gz - first, p.gz)
                after = a * p.gz + lax.rem(z + last, p.gz)
                left = series_of(u, before, p.rg, p.ta)
                right = series_of(u, after, p.rg, p.ta)
                b = a * p.gz + z
                both = jnp.where(lane % 4 < 2, left, right).astype(jnp.bfloat16)
                sides[b * p.nt : (b + 1) * p.nt, :] = both
        slope[...] = jnp.dot(sides[...], outer_ref[...], preferred_element_type=jnp.float32)

        def row_of(a, z, r):
            shift, r = divmod(r, p.rg)
            own = series_of(w, (a % p.gx) * p.gz + z, r, p.ta)
            if shift == 0:
                return own
            other = series_of(w, ((a + (1 if shift > 0 else -1)) % p.gx) * p.gz + z, r, p.ta)
            width = shift * p.cc
            if shift > 0:
                return pltpu.roll(jnp.where(lane < width, other, own), LANES - width, 1)
            return pltpu.roll(jnp.where(lane >= LANES + width, other, own), -width, 1)

        for a in range(p.gx):
            for z in range(p.gz):
                b = a * p.gz + z
                rows = {r: row_of(a, z, r) for r in range(-2, p.rg + 2)}
                for r in range(p.rg):
                    across = 8.0 * (rows[r + 1] - rows[r - 1]) - (rows[r + 2] - rows[r - 2])
                    mine = series_of(u, b, r, p.ta).astype(jnp.bfloat16)
                    along = jnp.dot(mine, inner_ref[...], preferred_element_type=jnp.float32)
                    along = along + slope[b * p.nt : (b + 1) * p.nt, r * LANES : (r + 1) * LANES]
                    spin = (along - across) / 12.0
                    for m in range(p.ta):
                        out[b, m, r] = spin[m * p.tl : (m + 1) * p.tl].astype(jnp.bfloat16)

    shape = (p.blocks, p.ta, p.rg, p.tl, LANES)
    whole = lambda x: pl.BlockSpec(x.shape, lambda i, s: (0,) * x.ndim)
    return pl.pallas_call(
        body,
        grid_spec=pltpu.PrefetchScalarGridSpec(
            num_scalar_prefetch=1,
            grid=(1,),
            in_specs=[whole(stream), whole(span), whole(inner), whole(outer)],
            out_specs=pl.BlockSpec(shape, lambda i, s: (0,) * 5),
            scratch_shapes=[
                pltpu.VMEM((p.blocks * p.nt, LANES), jnp.bfloat16),
                pltpu.VMEM((p.blocks * p.nt, p.rg * LANES), jnp.float32),
            ],
        ),
        out_shape=jax.ShapeDtypeStruct(shape, stream.dtype),
        name="vorticity",
    )(chunk, stream, span, inner, outer)


def cross(plan, series, rows, owner):
    p = plan
    scaling = 8.0 / (3.0 * SEG * NSEG)
    pair = 2 if p.rg % 2 == 0 else 1
    width = pair * LANES

    def body(owner_ref, x, table, out, spec, ref_spec):
        for r in range(0, p.rg, pair):
            slot = (r // pair) % 2
            for b in range(p.blocks):
                mine = jnp.concatenate([series_of(x, b, r + i, p.ta) for i in range(pair)], axis=1)
                spec[slot, b] = jnp.dot(
                    table[...], mine.astype(jnp.bfloat16), preferred_element_type=jnp.float32
                )
            for s in range(NSEG):
                at = s * ROWS
                ref_spec[slot, at : at + ROWS, :] = spec[slot, owner_ref[s], at : at + ROWS, :]
            for b in range(p.blocks):
                co = jnp.zeros((8, width), jnp.float32)
                quad = jnp.zeros((8, width), jnp.float32)
                for s in range(NSEG):
                    at = s * ROWS
                    rc, rs = ref_spec[slot, at : at + 8, :], ref_spec[slot, at + 8 : at + 16, :]
                    qc, qs = spec[slot, b, at : at + 8, :], spec[slot, b, at + 8 : at + 16, :]
                    co = co + (rc * qc + rs * qs)
                    quad = quad + (rc * qs - rs * qc)
                both = (jnp.concatenate([co, quad], axis=0) * scaling).astype(jnp.bfloat16)
                for i in range(pair):
                    out[b, r + i] = both[:, i * LANES : (i + 1) * LANES]

    shape = (p.blocks, p.rg, ROWS, LANES)
    return pl.pallas_call(
        body,
        grid_spec=pltpu.PrefetchScalarGridSpec(
            num_scalar_prefetch=1,
            grid=(1,),
            in_specs=[
                pl.BlockSpec(series.shape, lambda i, o: (0,) * 5),
                pl.BlockSpec(rows.shape, lambda i, o: (0, 0)),
            ],
            out_specs=pl.BlockSpec(shape, lambda i, o: (0,) * 4),
            scratch_shapes=[
                pltpu.VMEM((2, p.blocks, NSEG * ROWS, width), jnp.float32),
                pltpu.VMEM((2, NSEG * ROWS, width), jnp.float32),
            ],
        ),
        out_shape=jax.ShapeDtypeStruct(shape, jnp.bfloat16),
        name="cross",
    )(owner, series, rows)


def assemble(plan, pieces):
    p = plan
    quantities = len(pieces)
    if not p.fast:
        x = jnp.stack(pieces).reshape(quantities, p.blocks, p.rg, 2, 8, p.groups, p.cc)[:, :, :, :, :F]
        x = x.transpose(0, 3, 4, 5, 2, 1, 6).astype(jnp.float32)
        return x.reshape(quantities, 2, F, p.xb, p.cs)

    def body(*refs):
        ins, out, wide = refs[:quantities], refs[quantities], refs[quantities + 1]
        for q in range(quantities):
            @pl.when(pl.program_id(0) == q)
            def _():
                wide[...] = ins[q][...].astype(jnp.float32).reshape(p.blocks, p.rg * ROWS, LANES)

        for part in range(2):
            for k in range(F):
                for tile in range(p.cs // LANES):
                    arrays = [
                        wide[tile * p.groups + i, pl.ds(part * 8 + k, p.rg, stride=ROWS), :]
                        for i in range(p.groups)
                    ]
                    for g, block in enumerate(exchange_groups(arrays, p.cc)):
                        out[0, part, k, g * p.rg : (g + 1) * p.rg, tile * LANES : (tile + 1) * LANES] = block

    return pl.pallas_call(
        body,
        grid=(quantities,),
        in_specs=[pl.BlockSpec(x.shape, lambda q: (0,) * 4) for x in pieces],
        out_specs=pl.BlockSpec((1, 2, F, p.xb, p.cs), lambda q: (q, 0, 0, 0, 0)),
        scratch_shapes=[pltpu.VMEM((p.blocks, p.rg * ROWS, LANES), jnp.float32)],
        out_shape=jax.ShapeDtypeStruct((quantities, 2, F, p.xb, p.cs), jnp.float32),
        name="assemble",
    )(*pieces)


def shards(velocity, offsets, owner):
    plan = Plan(velocity)
    block = lax.axis_index(("gx", "gz")).astype(jnp.int32)
    chunk = lax.axis_index("ta").astype(jnp.int32) * plan.blocks + block

    def spread(quantity, edges):
        x = pack(plan, velocity, quantity, edges)
        x = x.reshape((-1,) + x.shape[2:])
        x = lax.all_to_all(x, ("gx", "gz", "ta"), split_axis=0, concat_axis=0, tiled=True)
        return x.reshape((plan.blocks, plan.ta) + x.shape[1:])

    def back(x):
        return lax.all_to_all(x, ("gx", "gz"), split_axis=0, concat_axis=0, tiled=True)

    table = dft_rows(offsets, jnp.arange(plan.nt, dtype=jnp.int32))
    span = spread(2, False)
    stream = spread(0, True)
    wall = spread(1, False)
    spin = vorticity(plan, stream, span, chunk.reshape(1))
    return assemble(plan, [back(cross(plan, x, table, owner)) for x in (stream, wall, span, spin)])


def solution(mesh):
    in_specs = (P(None, "ta", "gx", "gz"), P(), P())
    out_specs = P(None, None, None, "gx", ("gz", "ta"))
    return jax.shard_map(shards, mesh=mesh, in_specs=in_specs, out_specs=out_specs, check_vma=False)
```

```python
import math

import jax
import jax.numpy as jnp
import numpy as np
from jax import lax
from jax.experimental import pallas as pl
from jax.experimental.pallas import tpu as pltpu
from jax.sharding import PartitionSpec as P

SEG = 16
NSEG = 7
F = 7
ROWS = 16
LANES = 128


class Plan:
    def __init__(self, velocity):
        _, self.tl, self.xb, self.zb = velocity.shape
        self.gx, self.gz, self.ta = (lax.axis_size(a) for a in ("gx", "gz", "ta"))
        self.blocks = self.gx * self.gz
        self.nt = self.tl * self.ta
        self.cs = self.zb // self.ta
        self.cc = self.cs // self.blocks
        self.groups = LANES // self.cc
        self.rg = self.xb // self.groups
        self.chunks = self.zb // self.cc
        assert self.groups * self.rg == self.xb and self.xb * 4 == LANES and self.cc >= 2
        assert self.ta & (self.ta - 1) == 0
        self.fast = self.rg == 8 and self.tl == 8 and self.cs % LANES == 0


def dft_rows(offsets, times):
    lag = times[None, :] - offsets[:, None]
    inside = (lag >= 0) & (lag < SEG)
    window = 0.5 - 0.5 * jnp.cos((2.0 * math.pi / SEG) * lag.astype(jnp.float32))
    frequency = jnp.arange(1, 9, dtype=jnp.int32)
    turns = (frequency[None, :, None] * lag[:, None, :]) % SEG
    angle = (2.0 * math.pi / SEG) * turns.astype(jnp.float32)
    keep = inside[:, None, :] & (frequency <= F)[None, :, None]
    weight = jnp.where(keep, window[:, None, :], jnp.float32(0.0))
    rows = jnp.stack([weight * jnp.cos(angle), -weight * jnp.sin(angle)], axis=1)
    return rows.reshape(offsets.shape[0] * ROWS, times.shape[0]).astype(jnp.bfloat16)


def trade(x, axis, step):
    return lax.ppermute(x, axis, [(i, i ^ step) for i in range(lax.axis_size(axis))])


def exchange_groups(arrays, width):
    arrays = list(arrays)
    lane = lax.broadcasted_iota(jnp.int32, arrays[0].shape, 1)
    step = 1
    while step < len(arrays):
        odd = (lane & (width * step)) != 0
        for i in range(len(arrays)):
            if i & step == 0:
                a, b = arrays[i], arrays[i + step]
                arrays[i] = jnp.where(odd, pltpu.roll(b, width * step, 1), a)
                arrays[i + step] = jnp.where(odd, b, pltpu.roll(a, LANES - width * step, 1))
        step *= 2
    return arrays


def pack(plan, velocity, quantity, edges, place):
    p = plan
    shape = (p.blocks, p.ta, p.rg + (1 if edges else 0), p.tl, LANES)
    if not p.fast:
        x = velocity[quantity].reshape(p.tl, p.groups, p.rg, p.ta, p.blocks, p.cc)
        out = x.transpose(4, 3, 2, 0, 1, 5).reshape(p.blocks, p.ta, p.rg, p.tl, LANES)
        if edges:
            x = velocity[quantity].reshape(p.tl, p.xb, p.chunks, p.cc)
            before = jnp.roll(x[..., p.cc - 2 :], 1, axis=2)
            after = jnp.roll(x[..., :2], -1, axis=2)
            side = jnp.concatenate([before, after], axis=3).transpose(2, 0, 1, 3)
            side = side.reshape(p.ta, p.blocks, 1, p.tl, LANES).swapaxes(0, 1)
            out = jnp.concatenate([out, side], axis=2)
        return jnp.take(out, jnp.arange(p.ta, dtype=jnp.int32) ^ place[0], axis=1)
    per_slab = p.cs // LANES

    def body(place_ref, x, out, wide):
        for m in range(p.ta):
            slab = place_ref[0] ^ m
            for i in range(per_slab):
                at = pl.multiple_of(slab * p.cs + i * LANES, LANES)
                first = m * p.blocks + i * p.groups
                for t in range(p.tl):
                    rows = x[0, t, :, pl.ds(at, LANES)].astype(jnp.float32)
                    mine = exchange_groups(
                        [rows[g * p.rg : (g + 1) * p.rg] for g in range(p.groups)], p.cc
                    )
                    for g in range(p.groups):
                        wide[first + g, t * p.rg : (t + 1) * p.rg, :] = mine[g]
                for g in range(p.groups):
                    for r in range(p.rg):
                        series = wide[first + g, pl.ds(r, p.tl, stride=p.rg), :]
                        out[i * p.groups + g, m, r] = series.astype(jnp.bfloat16)
        if edges:
            slot = lax.broadcasted_iota(jnp.int32, (p.tl, LANES), 1) & (p.cc - 1)
            is_left = (slot & 3) < 2
            slot = slot >> 2

            def one_chunk(c, carry):
                def held(chunk):
                    return (place_ref[0] ^ (chunk // p.blocks)) * p.blocks + chunk % p.blocks

                before = held(lax.rem(c + p.chunks - 1, p.chunks))
                after = held(lax.rem(c + 1, p.chunks))
                acc = jnp.zeros((p.tl, LANES), jnp.float32)
                for r in range(p.rg):
                    left = wide[before, pl.ds(r, p.tl, stride=p.rg), :]
                    right = wide[after, pl.ds(r, p.tl, stride=p.rg), :]
                    left = pltpu.roll(left, (4 * r + 2 - p.cc) % LANES, 1)
                    right = pltpu.roll(right, 4 * r + 2, 1)
                    acc = jnp.where(slot == r, jnp.where(is_left, left, right), acc)
                out[c % p.blocks, place_ref[0] ^ (c // p.blocks), p.rg] = acc.astype(jnp.bfloat16)
                return carry

            lax.fori_loop(0, p.chunks, one_chunk, 0, unroll=4)

    return pl.pallas_call(
        body,
        grid_spec=pltpu.PrefetchScalarGridSpec(
            num_scalar_prefetch=1,
            grid=(1,),
            in_specs=[pl.BlockSpec((1, p.tl, p.xb, p.zb), lambda i, s: (quantity, 0, 0, 0))],
            out_specs=pl.BlockSpec(shape, lambda i, s: (0,) * 5),
            scratch_shapes=[pltpu.VMEM((p.chunks, p.tl * p.rg, LANES), jnp.float32)],
        ),
        out_shape=jax.ShapeDtypeStruct(shape, velocity.dtype),
        name="pack",
    )(place, velocity)


def slope_taps(plan):
    p = plan
    tap = {1: 8.0, -1: -8.0, 2: -1.0, -2: 1.0}
    inner = np.zeros((LANES, LANES), np.float32)
    outer = np.zeros((LANES, p.rg, LANES), np.float32)
    for g in range(p.groups):
        for c in range(p.cc):
            to = g * p.cc + c
            for ahead, weight in tap.items():
                at = c + ahead
                if 0 <= at < p.cc:
                    inner[g * p.cc + at, to] = weight
                else:
                    side = at + 2 if at < 0 else at - p.cc + 2
                    for r in range(p.rg):
                        outer[(g * p.rg + r) * 4 + side, r, to] = weight
    return jnp.asarray(inner, jnp.bfloat16), jnp.asarray(outer.reshape(LANES, -1), jnp.bfloat16)


def part_specs(plan, parts):
    if len(parts) == 1:
        return [pl.BlockSpec(parts[0].shape, lambda i, s: (0,) * 5)]
    _, _, rows, tl, lanes = parts[0].shape
    own = pl.BlockSpec((plan.blocks, 1, rows, tl, lanes), lambda i, s: (0,) * 5)
    return [own] + [pl.BlockSpec(x.shape, lambda i, s: (0,) * 4) for x in parts[1:]]


def series_of(refs, b, r):
    if len(refs) == 1:
        x = [refs[0][b, m, r] for m in range(refs[0].shape[1])]
    else:
        x = [refs[0][b, 0, r]] + [ref[b, r] for ref in refs[1:]]
    return jnp.concatenate([part.astype(jnp.float32) for part in x], axis=0)


def vorticity(plan, stream, span, chunk):
    p = plan
    inner, outer = slope_taps(p)

    def body(chunk_ref, *refs):
        u, w = refs[: len(stream)], refs[len(stream) : len(stream) + len(span)]
        inner_ref, outer_ref, out, sides, slope = refs[len(stream) + len(span) :]
        first = (chunk_ref[0] == 0).astype(jnp.int32)
        last = (chunk_ref[0] == p.chunks - 1).astype(jnp.int32)
        lane = lax.broadcasted_iota(jnp.int32, (p.nt, LANES), 1)
        for a in range(p.gx):
            for z in range(p.gz):
                before = a * p.gz + lax.rem(z + p.gz - first, p.gz)
                after = a * p.gz + lax.rem(z + last, p.gz)
                left = series_of(u, before, p.rg)
                right = series_of(u, after, p.rg)
                b = a * p.gz + z
                both = jnp.where(lane % 4 < 2, left, right).astype(jnp.bfloat16)
                sides[b * p.nt : (b + 1) * p.nt, :] = both
        slope[...] = jnp.dot(sides[...], outer_ref[...], preferred_element_type=jnp.float32)

        def row_of(a, z, r):
            shift, r = divmod(r, p.rg)
            own = series_of(w, (a % p.gx) * p.gz + z, r)
            if shift == 0:
                return own
            other = series_of(w, ((a + (1 if shift > 0 else -1)) % p.gx) * p.gz + z, r)
            width = shift * p.cc
            if shift > 0:
                return pltpu.roll(jnp.where(lane < width, other, own), LANES - width, 1)
            return pltpu.roll(jnp.where(lane >= LANES + width, other, own), -width, 1)

        for a in range(p.gx):
            for z in range(p.gz):
                b = a * p.gz + z
                rows = {r: row_of(a, z, r) for r in range(-2, p.rg + 2)}
                for r in range(p.rg):
                    across = 8.0 * (rows[r + 1] - rows[r - 1]) - (rows[r + 2] - rows[r - 2])
                    mine = series_of(u, b, r).astype(jnp.bfloat16)
                    along = jnp.dot(mine, inner_ref[...], preferred_element_type=jnp.float32)
                    along = along + slope[b * p.nt : (b + 1) * p.nt, r * LANES : (r + 1) * LANES]
                    spin = (along - across) / 12.0
                    for m in range(p.ta):
                        out[b, m, r] = spin[m * p.tl : (m + 1) * p.tl].astype(jnp.bfloat16)

    shape = (p.blocks, p.ta, p.rg, p.tl, LANES)
    whole = lambda x: pl.BlockSpec(x.shape, lambda i, s: (0,) * x.ndim)
    return pl.pallas_call(
        body,
        grid_spec=pltpu.PrefetchScalarGridSpec(
            num_scalar_prefetch=1,
            grid=(1,),
            in_specs=part_specs(p, stream) + part_specs(p, span) + [whole(inner), whole(outer)],
            out_specs=pl.BlockSpec(shape, lambda i, s: (0,) * 5),
            scratch_shapes=[
                pltpu.VMEM((p.blocks * p.nt, LANES), jnp.bfloat16),
                pltpu.VMEM((p.blocks * p.nt, p.rg * LANES), jnp.float32),
            ],
        ),
        out_shape=jax.ShapeDtypeStruct(shape, jnp.bfloat16),
        name="vorticity",
    )(chunk, *stream, *span, inner, outer)


def cross(plan, series, rows, owner):
    p = plan
    scaling = 8.0 / (3.0 * SEG * NSEG)
    pair = 2 if p.rg % 2 == 0 else 1
    width = pair * LANES

    def body(owner_ref, *refs):
        x = refs[: len(series)]
        table, out, spec, ref_spec = refs[len(series) :]
        for r in range(0, p.rg, pair):
            slot = (r // pair) % 2
            for b in range(p.blocks):
                mine = jnp.concatenate([series_of(x, b, r + i) for i in range(pair)], axis=1)
                spec[slot, b] = jnp.dot(
                    table[...], mine.astype(jnp.bfloat16), preferred_element_type=jnp.float32
                )
            for s in range(NSEG):
                at = s * ROWS
                ref_spec[slot, at : at + ROWS, :] = spec[slot, owner_ref[s], at : at + ROWS, :]
            for b in range(p.blocks):
                co = jnp.zeros((8, width), jnp.float32)
                quad = jnp.zeros((8, width), jnp.float32)
                for s in range(NSEG):
                    at = s * ROWS
                    rc, rs = ref_spec[slot, at : at + 8, :], ref_spec[slot, at + 8 : at + 16, :]
                    qc, qs = spec[slot, b, at : at + 8, :], spec[slot, b, at + 8 : at + 16, :]
                    co = co + (rc * qc + rs * qs)
                    quad = quad + (rc * qs - rs * qc)
                both = (jnp.concatenate([co, quad], axis=0) * scaling).astype(jnp.bfloat16)
                for i in range(pair):
                    out[b, r + i] = both[:, i * LANES : (i + 1) * LANES]

    shape = (p.blocks, p.rg, ROWS, LANES)
    return pl.pallas_call(
        body,
        grid_spec=pltpu.PrefetchScalarGridSpec(
            num_scalar_prefetch=1,
            grid=(1,),
            in_specs=part_specs(p, series) + [pl.BlockSpec(rows.shape, lambda i, o: (0, 0))],
            out_specs=pl.BlockSpec(shape, lambda i, o: (0,) * 4),
            scratch_shapes=[
                pltpu.VMEM((2, p.blocks, NSEG * ROWS, width), jnp.float32),
                pltpu.VMEM((2, NSEG * ROWS, width), jnp.float32),
            ],
        ),
        out_shape=jax.ShapeDtypeStruct(shape, jnp.bfloat16),
        name="cross",
    )(owner, *series, rows)


def assemble(plan, so_far, quantity, quantities, x):
    p = plan
    shape = (quantities, 2, F, p.xb, p.cs)
    if not p.fast:
        x = x.reshape(p.blocks, p.rg, 2, 8, p.groups, p.cc)[:, :, :, :F]
        x = x.transpose(2, 3, 4, 1, 0, 5).reshape(2, F, p.xb, p.cs).astype(jnp.float32)
        so_far = jnp.zeros(shape, jnp.float32) if so_far is None else so_far
        return so_far.at[quantity].set(x)

    def body(*refs):
        x, out, wide = refs[0], refs[-2], refs[-1]
        wide[...] = x[...].astype(jnp.float32).reshape(p.blocks, p.rg * ROWS, LANES)
        for part in range(2):
            for k in range(F):
                for tile in range(p.cs // LANES):
                    arrays = [
                        wide[tile * p.groups + i, pl.ds(part * 8 + k, p.rg, stride=ROWS), :]
                        for i in range(p.groups)
                    ]
                    for g, block in enumerate(exchange_groups(arrays, p.cc)):
                        out[0, part, k, g * p.rg : (g + 1) * p.rg, tile * LANES : (tile + 1) * LANES] = block

    before = [] if so_far is None else [so_far]
    return pl.pallas_call(
        body,
        grid=(1,),
        in_specs=[pl.BlockSpec(x.shape, lambda i: (0,) * 4)]
        + [pl.BlockSpec(memory_space=pl.ANY) for _ in before],
        out_specs=pl.BlockSpec((1, 2, F, p.xb, p.cs), lambda i: (quantity, 0, 0, 0, 0)),
        scratch_shapes=[pltpu.VMEM((p.blocks, p.rg * ROWS, LANES), jnp.float32)],
        out_shape=jax.ShapeDtypeStruct(shape, jnp.float32),
        input_output_aliases={1: 0} if before else {},
        name="assemble",
    )(x, *before)


def shards(velocity, offsets, owner):
    plan = Plan(velocity)
    block = lax.axis_index(("gx", "gz")).astype(jnp.int32)
    time = lax.axis_index("ta").astype(jnp.int32)
    chunk = (time * plan.blocks + block).reshape(1)
    place = time.reshape(1)

    def over_blocks(x):
        return lax.all_to_all(x, ("gx", "gz"), split_axis=0, concat_axis=0, tiled=True)

    def spread(quantity, edges):
        x = over_blocks(pack(plan, velocity, quantity, edges, place))
        return [x] + [trade(x[:, m], "ta", m) for m in range(1, plan.ta)]

    times = (jnp.arange(plan.ta, dtype=jnp.int32) ^ time)[:, None] * plan.tl
    times = (times + jnp.arange(plan.tl, dtype=jnp.int32)[None, :]).reshape(-1)
    table = dft_rows(offsets, times)
    span = spread(2, False)
    stream = spread(0, True)
    wall = spread(1, False)
    spin = [vorticity(plan, stream, span, chunk)]
    out = None
    for quantity, series in ((2, span), (0, stream), (3, spin), (1, wall)):
        out = assemble(plan, out, quantity, 4, over_blocks(cross(plan, series, table, owner)))
    return out


def solution(mesh):
    in_specs = (P(None, "ta", "gx", "gz"), P(), P())
    out_specs = P(None, None, None, "gx", ("gz", "ta"))
    return jax.shard_map(shards, mesh=mesh, in_specs=in_specs, out_specs=out_specs, check_vma=False)
```

```python
import math

import jax
import jax.numpy as jnp
import numpy as np
from jax import lax
from jax.experimental import pallas as pl
from jax.experimental.pallas import tpu as pltpu
from jax.sharding import PartitionSpec as P

SEG = 16
NSEG = 7
F = 7
ROWS = 16
LANES = 128
PARTNERS = 8


class Plan:
    def __init__(self, velocity):
        _, self.tl, self.xb, self.zb = velocity.shape
        self.gx, self.gz, self.ta = (lax.axis_size(a) for a in ("gx", "gz", "ta"))
        self.blocks = self.gx * self.gz
        self.nt = self.tl * self.ta
        self.cs = self.zb // self.ta
        self.cc = self.cs // self.blocks
        self.groups = LANES // self.cc
        self.rg = self.xb // self.groups
        self.chunks = self.zb // self.cc
        assert self.groups * self.rg == self.xb and self.xb * 4 == LANES and self.cc >= 2
        assert self.ta & (self.ta - 1) == 0 and self.blocks & (self.blocks - 1) == 0
        self.by_partner = self.blocks <= PARTNERS
        self.fast = self.rg == 8 and self.tl == 8 and self.cs % LANES == 0


def on_chip(body, inputs, outs, scratch, scalars=(), in_hbm=0, **params):
    count = len(inputs) - in_hbm
    arrays = [pltpu.with_memory_space_constraint(x, pltpu.VMEM) for x in inputs[:count]]
    if not params:
        arrays += [pltpu.with_memory_space_constraint(x, pltpu.HBM) for x in inputs[count:]]
    else:
        arrays += inputs[count:]
    vmem = pl.BlockSpec(memory_space=pltpu.VMEM)
    smem = pl.BlockSpec(memory_space=pltpu.SMEM)
    hbm = pl.BlockSpec(memory_space=pl.ANY)
    return pl.pallas_call(
        body,
        in_specs=[smem] * len(scalars) + [vmem] * count + [hbm] * in_hbm,
        out_specs=jax.tree.map(lambda x: hbm if isinstance(x, jax.ShapeDtypeStruct) else vmem, outs),
        out_shape=outs,
        scratch_shapes=scratch,
        compiler_params=pltpu.CompilerParams(vmem_limit_bytes=24 << 20),
        **params,
    )(*scalars, *arrays)


def dft_rows(offsets, times):
    lag = times[None, :] - offsets[:, None]
    inside = (lag >= 0) & (lag < SEG)
    window = 0.5 - 0.5 * jnp.cos((2.0 * math.pi / SEG) * lag.astype(jnp.float32))
    frequency = jnp.arange(1, 9, dtype=jnp.int32)
    turns = (frequency[None, :, None] * lag[:, None, :]) % SEG
    angle = (2.0 * math.pi / SEG) * turns.astype(jnp.float32)
    keep = inside[:, None, :] & (frequency <= F)[None, :, None]
    weight = jnp.where(keep, window[:, None, :], jnp.float32(0.0))
    rows = jnp.stack([weight * jnp.cos(angle), -weight * jnp.sin(angle)], axis=1)
    return rows.reshape(offsets.shape[0] * ROWS, times.shape[0]).astype(jnp.bfloat16)


def trade(x, axis, step, count):
    return lax.ppermute(x, axis, [(i, i ^ step) for i in range(count)])


def group_swap(plan):
    p = plan
    size = p.groups * p.groups * p.cc
    at = np.arange(size).reshape(p.groups, p.groups, p.cc)
    matrix = np.zeros((size, size), np.float32)
    matrix[at.reshape(-1), at.transpose(1, 0, 2).reshape(-1)] = 1.0
    return jnp.asarray(matrix, jnp.bfloat16)


def side_picks(plan):
    p = plan
    matrix = np.zeros((p.rg, p.groups, p.cc, 2, p.groups, p.rg, 4), np.float32)
    for r in range(p.rg):
        for g in range(p.groups):
            for n in range(2):
                matrix[r, g, p.cc - 2 + n, 0, g, r, n] = 1.0
                matrix[r, g, n, 1, g, r, 2 + n] = 1.0
    return jnp.asarray(matrix.reshape(p.rg * LANES, 2 * LANES), jnp.bfloat16)


def split_slabs(plan, velocity, quantity, place):
    p = plan

    def body(place_ref, velocity_ref, *rest):
        outs, sems = rest[:-1], rest[-1]
        copies = []
        for n, out in enumerate(outs):
            slab = place_ref[0] ^ (n + 1)
            columns = pl.ds(pl.multiple_of(slab * p.cs, LANES), p.cs)
            copies.append(pltpu.make_async_copy(velocity_ref.at[quantity, :, :, columns], out, sems.at[n]))
            copies[-1].start()
        for copy in copies:
            copy.wait()

    outs = [pltpu.VMEM((p.tl, p.xb, p.cs), velocity.dtype) for _ in range(1, p.ta)]
    scratch = [pltpu.SemaphoreType.DMA((p.ta - 1,))]
    return on_chip(body, [velocity], outs, scratch, (place,), in_hbm=1)


def rows_by_snapshot(plan, wide, tiles):
    p = plan
    lhs = []
    for g in range(p.groups):
        rows = [
            wide[tile, pl.ds(g * p.rg + r, p.tl, stride=p.xb), :] for tile in tiles for r in range(p.rg)
        ]
        lhs.append(jnp.concatenate(rows, axis=0).astype(jnp.bfloat16))
    return jnp.concatenate(lhs, axis=1)


def pack_slab(plan, velocity, quantity, arrived, place):
    p = plan
    shape = (p.ta, p.rg, p.tl, LANES)
    if not p.fast:
        own = lax.dynamic_slice_in_dim(velocity[quantity], place[0] * p.cs, p.cs, axis=2)
        x = jnp.stack([own] + list(arrived)).reshape(p.ta, p.tl, p.groups, p.rg, p.blocks, p.cc)
        x = x.transpose(4, 0, 3, 1, 2, 5).reshape((p.blocks,) + shape)
        return [jnp.take(x, place[1] ^ n, axis=0) for n in range(p.blocks)] if p.by_partner else [x]
    assert p.by_partner
    per_slab = p.cs // LANES

    def body(place_ref, swap, *rest):
        others, velocity_ref = rest[: p.ta - 1], rest[p.ta - 1]
        outs = rest[p.ta : p.ta + p.blocks]
        own, sem, wide, chunks = rest[p.ta + p.blocks :]
        columns = pl.ds(pl.multiple_of(place_ref[0] * p.cs, LANES), p.cs)
        copy = pltpu.make_async_copy(velocity_ref.at[quantity, :, :, columns], own, sem.at[0])
        copy.start()
        for m in list(range(1, p.ta)) + [0]:
            if m == 0:
                copy.wait()
            x = own if m == 0 else others[m - 1]
            for i in range(per_slab):
                rows = x[:, :, i * LANES : (i + 1) * LANES].astype(jnp.float32)
                wide[m * per_slab + i] = rows.reshape(p.tl * p.xb, LANES)
        tiles = range(p.ta * per_slab)
        swapped = jnp.dot(
            rows_by_snapshot(p, wide, tiles), swap[...], preferred_element_type=jnp.float32
        ).astype(jnp.bfloat16)
        count = p.rg * p.tl
        for tile in tiles:
            m, i = divmod(tile, per_slab)
            for g in range(p.groups):
                mine = swapped[tile * count : (tile + 1) * count, g * LANES : (g + 1) * LANES]
                chunks[i * p.groups + g, m] = mine.reshape(p.rg, p.tl, LANES)
        for n in range(p.blocks):
            outs[n][...] = chunks[place_ref[1] ^ n]

    outs = [pltpu.VMEM(shape, velocity.dtype) for _ in range(p.blocks)]
    scratch = [
        pltpu.VMEM((p.tl, p.xb, p.cs), velocity.dtype),
        pltpu.SemaphoreType.DMA((1,)),
        pltpu.VMEM((p.zb // LANES, p.tl * p.xb, LANES), jnp.float32),
        pltpu.VMEM((p.blocks,) + shape, velocity.dtype),
    ]
    return on_chip(body, [group_swap(p), *arrived, velocity], outs, scratch, (place,), in_hbm=1)


def pack_all(plan, velocity):
    p = plan
    shape = (p.blocks, p.ta, 2 * p.rg + 1, p.tl, LANES)
    if not p.fast:
        out = []
        for quantity in (2, 0):
            x = velocity[quantity].reshape(p.tl, p.groups, p.rg, p.ta, p.blocks, p.cc)
            out.append(x.transpose(4, 3, 2, 0, 1, 5).reshape(p.blocks, p.ta, p.rg, p.tl, LANES))
        x = velocity[0].reshape(p.tl, p.xb, p.chunks, p.cc)
        before = jnp.roll(x[..., p.cc - 2 :], 1, axis=2)
        after = jnp.roll(x[..., :2], -1, axis=2)
        side = jnp.concatenate([before, after], axis=3).transpose(2, 0, 1, 3)
        out.append(side.reshape(p.ta, p.blocks, 1, p.tl, LANES).swapaxes(0, 1))
        return jnp.concatenate(out, axis=2)
    per_slab = p.cs // LANES
    half = max(p.ta // 2, 1)

    def body(swap_hbm, picks_hbm, velocity_ref, out, x, sems, table_sems, wide, swap, picks, chunks):
        tables = [
            pltpu.make_async_copy(swap_hbm, swap, table_sems.at[0]),
            pltpu.make_async_copy(picks_hbm, picks, table_sems.at[1]),
        ]
        tables[0].start()
        copies = {}
        for n, quantity in enumerate((2, 0)):
            for start in range(0, p.ta, half):
                columns = slice(start * p.cs, (start + half) * p.cs)
                copies[n, start] = pltpu.make_async_copy(
                    velocity_ref.at[quantity, :, :, columns], x.at[n, :, :, columns], sems.at[n, start]
                )
                copies[n, start].start()
        tables[1].start()
        tables[0].wait()
        count = p.rg * p.tl
        for n in range(2):
            for start in range(0, p.ta, half):
                copies[n, start].wait()
                tiles = range(start * per_slab, (start + half) * per_slab)
                for tile in tiles:
                    rows = x[n, :, :, tile * LANES : (tile + 1) * LANES].astype(jnp.float32)
                    wide[tile] = rows.reshape(p.tl * p.xb, LANES)
                swapped = jnp.dot(
                    rows_by_snapshot(p, wide, tiles), swap[...], preferred_element_type=jnp.float32
                )
                for tile in tiles:
                    at = (tile - tiles[0]) * count
                    m, i = divmod(tile, per_slab)
                    for g in range(p.groups):
                        mine = swapped[at : at + count, g * LANES : (g + 1) * LANES]
                        if n == 1:
                            chunks[tile * p.groups + g] = mine
                        out[i * p.groups + g, m, n * p.rg : (n + 1) * p.rg] = mine.reshape(
                            p.rg, p.tl, LANES
                        ).astype(jnp.bfloat16)
        tables[1].wait()
        acc = jnp.zeros((p.chunks * p.tl, 2 * LANES), jnp.float32)
        for r in range(p.rg):
            rows = [chunks[c, r * p.tl : (r + 1) * p.tl, :] for c in range(p.chunks)]
            acc = acc + jnp.dot(
                jnp.concatenate(rows, axis=0).astype(jnp.bfloat16),
                picks[r * LANES : (r + 1) * LANES, :],
                preferred_element_type=jnp.float32,
            )
        for c in range(p.chunks):
            before, after = (c + p.chunks - 1) % p.chunks, (c + 1) % p.chunks
            both = (
                acc[before * p.tl : (before + 1) * p.tl, :LANES]
                + acc[after * p.tl : (after + 1) * p.tl, LANES:]
            )
            out[c % p.blocks, c // p.blocks, 2 * p.rg] = both.astype(jnp.bfloat16)

    swap, picks = group_swap(p), side_picks(p)
    scratch = [
        pltpu.VMEM((2, p.tl, p.xb, p.zb), velocity.dtype),
        pltpu.SemaphoreType.DMA((2, p.ta)),
        pltpu.SemaphoreType.DMA((2,)),
        pltpu.VMEM((p.zb // LANES, p.tl * p.xb, LANES), jnp.float32),
        pltpu.VMEM(swap.shape, swap.dtype),
        pltpu.VMEM(picks.shape, picks.dtype),
        pltpu.VMEM((p.chunks, p.rg * p.tl, LANES), jnp.float32),
    ]
    outs = pltpu.VMEM(shape, velocity.dtype)
    return on_chip(body, [swap, picks, velocity], outs, scratch, in_hbm=3)


def slope_taps(plan):
    p = plan
    tap = {1: 8.0, -1: -8.0, 2: -1.0, -2: 1.0}
    inner = np.zeros((LANES, LANES), np.float32)
    outer = np.zeros((LANES, p.rg, LANES), np.float32)
    for g in range(p.groups):
        for c in range(p.cc):
            to = g * p.cc + c
            for ahead, weight in tap.items():
                at = c + ahead
                if 0 <= at < p.cc:
                    inner[g * p.cc + at, to] = weight
                else:
                    side = at + 2 if at < 0 else at - p.cc + 2
                    for r in range(p.rg):
                        outer[(g * p.rg + r) * 4 + side, r, to] = weight
    return jnp.asarray(inner, jnp.bfloat16), jnp.asarray(outer.reshape(LANES, -1), jnp.bfloat16)


def series_of(ref, b, r):
    x = [ref[b, m, r].astype(jnp.float32) for m in range(ref.shape[1])]
    return jnp.concatenate(x, axis=0)


def vorticity(plan, both, place):
    p = plan
    inner, outer = slope_taps(p)

    def body(place_ref, x, inner_ref, outer_ref, out, sides, slope):
        chunk = place_ref[0] * p.blocks + place_ref[1]
        first = (chunk == 0).astype(jnp.int32)
        last = (chunk == p.chunks - 1).astype(jnp.int32)
        lane = lax.broadcasted_iota(jnp.int32, (p.nt, LANES), 1)
        for a in range(p.gx):
            for z in range(p.gz):
                before = a * p.gz + lax.rem(z + p.gz - first, p.gz)
                after = a * p.gz + lax.rem(z + last, p.gz)
                left = series_of(x, before, 2 * p.rg)
                right = series_of(x, after, 2 * p.rg)
                b = a * p.gz + z
                side = jnp.where(lane % 4 < 2, left, right).astype(jnp.bfloat16)
                sides[b * p.nt : (b + 1) * p.nt, :] = side
        slope[...] = jnp.dot(sides[...], outer_ref[...], preferred_element_type=jnp.float32)

        def row_of(a, z, r):
            shift, r = divmod(r, p.rg)
            own = series_of(x, (a % p.gx) * p.gz + z, r)
            if shift == 0:
                return own
            other = series_of(x, ((a + (1 if shift > 0 else -1)) % p.gx) * p.gz + z, r)
            width = shift * p.cc
            if shift > 0:
                return pltpu.roll(jnp.where(lane < width, other, own), LANES - width, 1)
            return pltpu.roll(jnp.where(lane >= LANES + width, other, own), -width, 1)

        for a in range(p.gx):
            for z in range(p.gz):
                b = a * p.gz + z
                rows = {r: row_of(a, z, r) for r in range(-2, p.rg + 2)}
                for r in range(p.rg):
                    across = 8.0 * (rows[r + 1] - rows[r - 1]) - (rows[r + 2] - rows[r - 2])
                    mine = series_of(x, b, p.rg + r).astype(jnp.bfloat16)
                    along = jnp.dot(mine, inner_ref[...], preferred_element_type=jnp.float32)
                    along = along + slope[b * p.nt : (b + 1) * p.nt, r * LANES : (r + 1) * LANES]
                    spin = (along - across) / 12.0
                    for m in range(p.ta):
                        out[b, m, r] = spin[m * p.tl : (m + 1) * p.tl].astype(jnp.bfloat16)

    outs = pltpu.VMEM((p.blocks, p.ta, p.rg, p.tl, LANES), jnp.bfloat16)
    scratch = [
        pltpu.VMEM((p.blocks * p.nt, LANES), jnp.bfloat16),
        pltpu.VMEM((p.blocks * p.nt, p.rg * LANES), jnp.float32),
    ]
    return on_chip(body, [both, inner, outer], outs, scratch, (place,))


def cross(plan, series, starts, table, owner, place, by_partner):
    p = plan
    scaling = 8.0 / (3.0 * SEG * NSEG)
    pair = 2 if p.rg % 2 == 0 else 1
    width = pair * LANES
    split = len(series) > 1

    def body(owner_ref, place_ref, *refs):
        xs, table_ref = refs[: len(series)], refs[len(series)]
        outs, (spec, ref_spec) = refs[len(series) + 1 : -2], refs[-2:]
        turn = 0
        for q, start in enumerate(starts):
            for r in range(0, p.rg, pair):
                slot = turn % 2
                turn += 1
                for n in range(p.blocks):
                    rows = []
                    for i in range(pair):
                        at = start + r + i
                        if split:
                            x = [xs[n][m, at].astype(jnp.float32) for m in range(p.ta)]
                            rows.append(jnp.concatenate(x, axis=0))
                        else:
                            rows.append(series_of(xs[0], n, at))
                    b = place_ref[1] ^ n if split else n
                    spec[slot, b] = jnp.dot(
                        table_ref[...],
                        jnp.concatenate(rows, axis=1).astype(jnp.bfloat16),
                        preferred_element_type=jnp.float32,
                    )
                for s in range(NSEG):
                    at = s * ROWS
                    ref_spec[slot, at : at + ROWS, :] = spec[slot, owner_ref[s], at : at + ROWS, :]
                for n in range(p.blocks):
                    b = place_ref[1] ^ n if by_partner else n
                    co = jnp.zeros((8, width), jnp.float32)
                    quad = jnp.zeros((8, width), jnp.float32)
                    for s in range(NSEG):
                        at = s * ROWS
                        rc, rs = ref_spec[slot, at : at + 8, :], ref_spec[slot, at + 8 : at + 16, :]
                        qc, qs = spec[slot, b, at : at + 8, :], spec[slot, b, at + 8 : at + 16, :]
                        co = co + (rc * qc + rs * qs)
                        quad = quad + (rc * qs - rs * qc)
                    both = (jnp.concatenate([co, quad], axis=0) * scaling).astype(jnp.bfloat16)
                    for i in range(pair):
                        mine = both[:, i * LANES : (i + 1) * LANES]
                        if by_partner:
                            outs[n][q, r + i] = mine
                        else:
                            outs[0][n, q, r + i] = mine

    shape = (len(starts), p.rg, ROWS, LANES)
    if by_partner:
        outs = [pltpu.VMEM(shape, jnp.bfloat16) for _ in range(p.blocks)]
    else:
        outs = [pltpu.VMEM((p.blocks,) + shape, jnp.bfloat16)]
    scratch = [
        pltpu.VMEM((2, p.blocks, NSEG * ROWS, width), jnp.float32),
        pltpu.VMEM((2, NSEG * ROWS, width), jnp.float32),
    ]
    return on_chip(body, [*series, table], outs, scratch, (owner, place))


def assemble(plan, so_far, quantities, pieces, place):
    p = plan
    shape = (4, 2, F, p.xb, p.cs)
    if not p.fast:
        if len(pieces) > 1:
            x = jnp.stack(pieces)
            x = jnp.take(x, jnp.arange(p.blocks, dtype=jnp.int32) ^ place[1], axis=0)
        else:
            x = pieces[0]
        out = jnp.zeros(shape, jnp.float32) if so_far is None else so_far
        x = x.reshape(p.blocks, len(quantities), p.rg, 2, 8, p.groups, p.cc)[:, :, :, :, :F]
        x = x.transpose(1, 3, 4, 5, 2, 0, 6).reshape((-1,) + shape[1:]).astype(jnp.float32)
        for n, quantity in enumerate(quantities):
            out = out.at[quantity].set(x[n])
        return out

    def body(place_ref, *refs):
        xs, swap = refs[: len(pieces)], refs[len(pieces)]
        out, by_chunk, wide, held, sems = refs[-5:]
        copies = []
        for n, quantity in enumerate(quantities):
            for j in range(p.blocks):
                if len(pieces) > 1:
                    by_chunk[place_ref[1] ^ j] = xs[j][n].reshape(p.rg * ROWS, LANES)
                else:
                    by_chunk[j] = xs[0][j, n].reshape(p.rg * ROWS, LANES)
            for tile in range(p.cs // LANES):
                lhs = [by_chunk[tile * p.groups + i] for i in range(p.groups)]
                swapped = jnp.dot(
                    jnp.concatenate(lhs, axis=1), swap[...], preferred_element_type=jnp.float32
                )
                for g in range(p.groups):
                    wide[tile, g] = swapped[:, g * LANES : (g + 1) * LANES]
            for part in range(2):
                for k in range(F):
                    for tile in range(p.cs // LANES):
                        for g in range(p.groups):
                            block = wide[tile, g, pl.ds(part * 8 + k, p.rg, stride=ROWS), :]
                            rows = slice(g * p.rg, (g + 1) * p.rg)
                            held[n, part, k, rows, tile * LANES : (tile + 1) * LANES] = block
                copies.append(
                    pltpu.make_async_copy(held.at[n, part], out.at[quantity, part], sems.at[n, part])
                )
                copies[-1].start()
        for copy in copies:
            copy.wait()

    before = [] if so_far is None else [so_far]
    scratch = [
        pltpu.VMEM((p.blocks, p.rg * ROWS, LANES), jnp.bfloat16),
        pltpu.VMEM((p.cs // LANES, p.groups, p.rg * ROWS, LANES), jnp.float32),
        pltpu.VMEM((len(quantities),) + shape[1:], jnp.float32),
        pltpu.SemaphoreType.DMA((len(quantities), 2)),
    ]
    return on_chip(
        body,
        [*pieces, group_swap(p)] + before,
        jax.ShapeDtypeStruct(shape, jnp.float32),
        scratch,
        (place,),
        in_hbm=len(before),
        **({"input_output_aliases": {len(pieces) + 2: 0}} if before else {}),
    )


def shards(velocity, offsets, owner):
    plan = Plan(velocity)
    block_axes = ("gx", "gz")
    time = lax.axis_index("ta").astype(jnp.int32)
    place = jnp.stack([time, lax.axis_index(block_axes).astype(jnp.int32)])

    slabs = split_slabs(plan, velocity, 1, place)
    slabs = [trade(x, "ta", n + 1, plan.ta) for n, x in enumerate(slabs)]
    both = pack_all(plan, velocity)
    both = both.reshape((-1,) + both.shape[2:])
    both = lax.all_to_all(both, block_axes + ("ta",), split_axis=0, concat_axis=0, tiled=True)
    both = both.reshape((plan.blocks, plan.ta) + both.shape[1:])

    def over_blocks(arrays):
        if len(arrays) == 1:
            return [lax.all_to_all(arrays[0], block_axes, split_axis=0, concat_axis=0, tiled=True)]
        return [arrays[0]] + [trade(arrays[n], block_axes, n, plan.blocks) for n in range(1, plan.blocks)]

    wall = pack_slab(plan, velocity, 1, slabs, place)
    wall = over_blocks(wall)
    times = jnp.arange(plan.tl, dtype=jnp.int32)[None, :]
    turn = jnp.arange(plan.ta, dtype=jnp.int32)[:, None]
    table_wall = dft_rows(offsets, ((turn ^ time) * plan.tl + times).reshape(-1))
    table = dft_rows(offsets, (turn * plan.tl + times).reshape(-1))
    wall = cross(plan, wall, (0,), table_wall, owner, place, plan.by_partner)
    wall = over_blocks(wall)
    out = assemble(plan, None, (1,), wall, place)

    pieces = cross(plan, [both], (0, plan.rg), table, owner, place, False)
    pieces = over_blocks(pieces)
    spin = vorticity(plan, both, place)
    spin = cross(plan, [spin], (0,), table, owner, place, plan.by_partner)
    spin = over_blocks(spin)
    out = assemble(plan, out, (2, 0), pieces, place)
    return assemble(plan, out, (3,), spin, place)


def solution(mesh):
    in_specs = (P(None, "ta", "gx", "gz"), P(), P())
    out_specs = P(None, None, None, "gx", ("gz", "ta"))

    return jax.shard_map(shards, mesh=mesh, in_specs=in_specs, out_specs=out_specs, check_vma=False)
```

```python
import math

import jax
import jax.numpy as jnp
import numpy as np
from jax import lax
from jax.experimental import pallas as pl
from jax.experimental.pallas import tpu as pltpu
from jax.sharding import PartitionSpec as P

SEG = 16
NSEG = 7
F = 7
ROWS = 16
LANES = 128
PARTNERS = 8


class Plan:
    def __init__(self, velocity):
        _, self.tl, self.xb, self.zb = velocity.shape
        self.gx, self.gz, self.ta = (lax.axis_size(a) for a in ("gx", "gz", "ta"))
        self.blocks = self.gx * self.gz
        self.nt = self.tl * self.ta
        self.cs = self.zb // self.ta
        self.cc = self.cs // self.blocks
        self.groups = LANES // self.cc
        self.rg = self.xb // self.groups
        self.chunks = self.zb // self.cc
        assert self.groups * self.rg == self.xb and self.xb * 4 == LANES and self.cc >= 2
        assert self.ta & (self.ta - 1) == 0 and self.blocks & (self.blocks - 1) == 0
        self.by_partner = self.blocks <= PARTNERS
        self.fast = self.rg == 8 and self.tl == 8 and self.cs % LANES == 0


def on_chip(body, inputs, outs, scratch, scalars=(), in_hbm=0, **params):
    count = len(inputs) - in_hbm
    arrays = [pltpu.with_memory_space_constraint(x, pltpu.VMEM) for x in inputs[:count]]
    if not params:
        arrays += [pltpu.with_memory_space_constraint(x, pltpu.HBM) for x in inputs[count:]]
    else:
        arrays += inputs[count:]
    vmem = pl.BlockSpec(memory_space=pltpu.VMEM)
    smem = pl.BlockSpec(memory_space=pltpu.SMEM)
    hbm = pl.BlockSpec(memory_space=pl.ANY)
    return pl.pallas_call(
        body,
        in_specs=[smem] * len(scalars) + [vmem] * count + [hbm] * in_hbm,
        out_specs=jax.tree.map(lambda x: hbm if isinstance(x, jax.ShapeDtypeStruct) else vmem, outs),
        out_shape=outs,
        scratch_shapes=scratch,
        compiler_params=pltpu.CompilerParams(vmem_limit_bytes=24 << 20),
        **params,
    )(*scalars, *arrays)


def dft_rows(offsets, times):
    lag = times[None, :] - offsets[:, None]
    inside = (lag >= 0) & (lag < SEG)
    window = 0.5 - 0.5 * jnp.cos((2.0 * math.pi / SEG) * lag.astype(jnp.float32))
    frequency = jnp.arange(1, 9, dtype=jnp.int32)
    turns = (frequency[None, :, None] * lag[:, None, :]) % SEG
    angle = (2.0 * math.pi / SEG) * turns.astype(jnp.float32)
    keep = inside[:, None, :] & (frequency <= F)[None, :, None]
    weight = jnp.where(keep, window[:, None, :], jnp.float32(0.0))
    rows = jnp.stack([weight * jnp.cos(angle), -weight * jnp.sin(angle)], axis=1)
    return rows.reshape(offsets.shape[0] * ROWS, times.shape[0]).astype(jnp.bfloat16)


def trade(x, axis, step, count):
    return lax.ppermute(x, axis, [(i, i ^ step) for i in range(count)])


def group_swap(plan):
    p = plan
    size = p.groups * p.groups * p.cc
    at = np.arange(size).reshape(p.groups, p.groups, p.cc)
    matrix = np.zeros((size, size), np.float32)
    matrix[at.reshape(-1), at.transpose(1, 0, 2).reshape(-1)] = 1.0
    return jnp.asarray(matrix, jnp.bfloat16)


def side_picks(plan):
    p = plan
    matrix = np.zeros((p.rg, p.groups, p.cc, 2, p.groups, p.rg, 4), np.float32)
    for r in range(p.rg):
        for g in range(p.groups):
            for n in range(2):
                matrix[r, g, p.cc - 2 + n, 0, g, r, n] = 1.0
                matrix[r, g, n, 1, g, r, 2 + n] = 1.0
    return jnp.asarray(matrix.reshape(p.rg * LANES, 2 * LANES), jnp.bfloat16)


def spread_rows(plan, wide, tile, rows):
    p = plan
    rows = rows.astype(jnp.float32)
    for g in range(p.groups):
        wide[tile, g] = rows[:, g * p.rg : (g + 1) * p.rg].reshape(p.tl * p.rg, LANES)


def rows_by_snapshot(plan, wide, tiles):
    p = plan
    lhs = []
    for g in range(p.groups):
        rows = [wide[tile, g, pl.ds(r, p.tl, stride=p.rg), :] for tile in tiles for r in range(p.rg)]
        lhs.append(jnp.concatenate(rows, axis=0).astype(jnp.bfloat16))
    return jnp.concatenate(lhs, axis=1)


def pack_one(plan, velocity, quantity, place):
    p = plan
    shape = (p.ta, p.rg, p.tl, LANES)
    if not p.by_partner or not p.fast:
        x = velocity[quantity].reshape(p.tl, p.groups, p.rg, p.ta, p.blocks, p.cc)
        x = x.transpose(4, 3, 2, 0, 1, 5).reshape((p.blocks,) + shape)
        x = jnp.take(x, jnp.arange(p.ta, dtype=jnp.int32) ^ place[0], axis=1)
        return [jnp.take(x, place[1] ^ n, axis=0) for n in range(p.blocks)] if p.by_partner else [x]
    per_slab = p.cs // LANES

    def body(place_ref, swap, velocity_ref, *rest):
        outs = rest[: p.blocks]
        x, sems, wide, chunks = rest[p.blocks :]
        copies = []
        for m in range(p.ta):
            columns = pl.ds(pl.multiple_of((place_ref[0] ^ m) * p.cs, LANES), p.cs)
            copies.append(
                pltpu.make_async_copy(velocity_ref.at[quantity, :, :, columns], x.at[m], sems.at[m])
            )
            copies[-1].start()
        for m in range(p.ta):
            copies[m].wait()
            for i in range(per_slab):
                spread_rows(p, wide, m * per_slab + i, x[m, :, :, i * LANES : (i + 1) * LANES])
        tiles = range(p.ta * per_slab)
        swapped = jnp.dot(
            rows_by_snapshot(p, wide, tiles), swap[...], preferred_element_type=jnp.float32
        ).astype(jnp.bfloat16)
        count = p.rg * p.tl
        for tile in tiles:
            m, i = divmod(tile, per_slab)
            for g in range(p.groups):
                mine = swapped[tile * count : (tile + 1) * count, g * LANES : (g + 1) * LANES]
                chunks[i * p.groups + g, m] = mine.reshape(p.rg, p.tl, LANES)
        for n in range(p.blocks):
            outs[n][...] = chunks[place_ref[1] ^ n]

    outs = [pltpu.VMEM(shape, velocity.dtype) for _ in range(p.blocks)]
    scratch = [
        pltpu.VMEM((p.ta, p.tl, p.xb, p.cs), velocity.dtype),
        pltpu.SemaphoreType.DMA((p.ta,)),
        pltpu.VMEM((p.zb // LANES, p.groups, p.tl * p.rg, LANES), jnp.float32),
        pltpu.VMEM((p.blocks,) + shape, velocity.dtype),
    ]
    return on_chip(body, [group_swap(p), velocity], outs, scratch, (place,), in_hbm=1)


def regroup(plan, arrays):
    p = plan
    if len(arrays) == 1:
        return [arrays[0][:, m] for m in range(p.ta)]

    def body(*refs):
        for n in range(p.blocks):
            for m in range(p.ta):
                refs[p.blocks + m][n] = refs[n][m]

    outs = [pltpu.VMEM((p.blocks, p.rg, p.tl, LANES), arrays[0].dtype) for _ in range(p.ta)]
    return on_chip(body, list(arrays), outs, [])


def pack_all(plan, velocity):
    p = plan
    shape = (p.blocks, p.ta, 2 * p.rg + 1, p.tl, LANES)
    if not p.fast:
        out = []
        for quantity in (2, 0):
            x = velocity[quantity].reshape(p.tl, p.groups, p.rg, p.ta, p.blocks, p.cc)
            out.append(x.transpose(4, 3, 2, 0, 1, 5).reshape(p.blocks, p.ta, p.rg, p.tl, LANES))
        x = velocity[0].reshape(p.tl, p.xb, p.chunks, p.cc)
        before = jnp.roll(x[..., p.cc - 2 :], 1, axis=2)
        after = jnp.roll(x[..., :2], -1, axis=2)
        side = jnp.concatenate([before, after], axis=3).transpose(2, 0, 1, 3)
        out.append(side.reshape(p.ta, p.blocks, 1, p.tl, LANES).swapaxes(0, 1))
        return jnp.concatenate(out, axis=2)
    per_slab = p.cs // LANES
    half = max(p.ta // 2, 1)

    def body(swap_hbm, picks_hbm, velocity_ref, out, x, sems, table_sems, wide, swap, picks, chunks):
        tables = [
            pltpu.make_async_copy(swap_hbm, swap, table_sems.at[0]),
            pltpu.make_async_copy(picks_hbm, picks, table_sems.at[1]),
        ]
        tables[0].start()
        copies = {}
        for n, quantity in enumerate((2, 0)):
            for start in range(0, p.ta, half):
                columns = slice(start * p.cs, (start + half) * p.cs)
                copies[n, start] = pltpu.make_async_copy(
                    velocity_ref.at[quantity, :, :, columns], x.at[n, :, :, columns], sems.at[n, start]
                )
                copies[n, start].start()
        tables[1].start()
        tables[0].wait()
        count = p.rg * p.tl
        for n in range(2):
            for start in range(0, p.ta, half):
                copies[n, start].wait()
                tiles = range(start * per_slab, (start + half) * per_slab)
                for tile in tiles:
                    spread_rows(p, wide, tile, x[n, :, :, tile * LANES : (tile + 1) * LANES])
                swapped = jnp.dot(
                    rows_by_snapshot(p, wide, tiles), swap[...], preferred_element_type=jnp.float32
                )
                for tile in tiles:
                    at = (tile - tiles[0]) * count
                    m, i = divmod(tile, per_slab)
                    for g in range(p.groups):
                        mine = swapped[at : at + count, g * LANES : (g + 1) * LANES]
                        if n == 1:
                            chunks[tile * p.groups + g] = mine
                        out[i * p.groups + g, m, n * p.rg : (n + 1) * p.rg] = mine.reshape(
                            p.rg, p.tl, LANES
                        ).astype(jnp.bfloat16)
        tables[1].wait()
        acc = jnp.zeros((p.chunks * p.tl, 2 * LANES), jnp.float32)
        for r in range(p.rg):
            rows = [chunks[c, r * p.tl : (r + 1) * p.tl, :] for c in range(p.chunks)]
            acc = acc + jnp.dot(
                jnp.concatenate(rows, axis=0).astype(jnp.bfloat16),
                picks[r * LANES : (r + 1) * LANES, :],
                preferred_element_type=jnp.float32,
            )
        for c in range(p.chunks):
            before, after = (c + p.chunks - 1) % p.chunks, (c + 1) % p.chunks
            both = (
                acc[before * p.tl : (before + 1) * p.tl, :LANES]
                + acc[after * p.tl : (after + 1) * p.tl, LANES:]
            )
            out[c % p.blocks, c // p.blocks, 2 * p.rg] = both.astype(jnp.bfloat16)

    swap, picks = group_swap(p), side_picks(p)
    scratch = [
        pltpu.VMEM((2, p.tl, p.xb, p.zb), velocity.dtype),
        pltpu.SemaphoreType.DMA((2, p.ta)),
        pltpu.SemaphoreType.DMA((2,)),
        pltpu.VMEM((p.zb // LANES, p.groups, p.tl * p.rg, LANES), jnp.float32),
        pltpu.VMEM(swap.shape, swap.dtype),
        pltpu.VMEM(picks.shape, picks.dtype),
        pltpu.VMEM((p.chunks, p.rg * p.tl, LANES), jnp.float32),
    ]
    outs = pltpu.VMEM(shape, velocity.dtype)
    return on_chip(body, [swap, picks, velocity], outs, scratch, in_hbm=3)


def slope_taps(plan):
    p = plan
    tap = {1: 8.0, -1: -8.0, 2: -1.0, -2: 1.0}
    inner = np.zeros((LANES, LANES), np.float32)
    outer = np.zeros((LANES, p.rg, LANES), np.float32)
    for g in range(p.groups):
        for c in range(p.cc):
            to = g * p.cc + c
            for ahead, weight in tap.items():
                at = c + ahead
                if 0 <= at < p.cc:
                    inner[g * p.cc + at, to] = weight
                else:
                    side = at + 2 if at < 0 else at - p.cc + 2
                    for r in range(p.rg):
                        outer[(g * p.rg + r) * 4 + side, r, to] = weight
    return jnp.asarray(inner, jnp.bfloat16), jnp.asarray(outer.reshape(LANES, -1), jnp.bfloat16)


def series_of(ref, b, r):
    x = [ref[b, m, r].astype(jnp.float32) for m in range(ref.shape[1])]
    return jnp.concatenate(x, axis=0)


def vorticity(plan, both, place):
    p = plan
    inner, outer = slope_taps(p)

    def body(place_ref, x, inner_ref, outer_ref, out, sides, slope):
        chunk = place_ref[0] * p.blocks + place_ref[1]
        first = (chunk == 0).astype(jnp.int32)
        last = (chunk == p.chunks - 1).astype(jnp.int32)
        lane = lax.broadcasted_iota(jnp.int32, (p.nt, LANES), 1)
        for a in range(p.gx):
            for z in range(p.gz):
                before = a * p.gz + lax.rem(z + p.gz - first, p.gz)
                after = a * p.gz + lax.rem(z + last, p.gz)
                left = series_of(x, before, 2 * p.rg)
                right = series_of(x, after, 2 * p.rg)
                b = a * p.gz + z
                side = jnp.where(lane % 4 < 2, left, right).astype(jnp.bfloat16)
                sides[b * p.nt : (b + 1) * p.nt, :] = side
        slope[...] = jnp.dot(sides[...], outer_ref[...], preferred_element_type=jnp.float32)

        def row_of(a, z, r):
            shift, r = divmod(r, p.rg)
            own = series_of(x, (a % p.gx) * p.gz + z, r)
            if shift == 0:
                return own
            other = series_of(x, ((a + (1 if shift > 0 else -1)) % p.gx) * p.gz + z, r)
            width = shift * p.cc
            if shift > 0:
                return pltpu.roll(jnp.where(lane < width, other, own), LANES - width, 1)
            return pltpu.roll(jnp.where(lane >= LANES + width, other, own), -width, 1)

        for a in range(p.gx):
            for z in range(p.gz):
                b = a * p.gz + z
                rows = {r: row_of(a, z, r) for r in range(-2, p.rg + 2)}
                for r in range(p.rg):
                    across = 8.0 * (rows[r + 1] - rows[r - 1]) - (rows[r + 2] - rows[r - 2])
                    mine = series_of(x, b, p.rg + r).astype(jnp.bfloat16)
                    along = jnp.dot(mine, inner_ref[...], preferred_element_type=jnp.float32)
                    along = along + slope[b * p.nt : (b + 1) * p.nt, r * LANES : (r + 1) * LANES]
                    spin = (along - across) / 12.0
                    for m in range(p.ta):
                        out[b, m, r] = spin[m * p.tl : (m + 1) * p.tl].astype(jnp.bfloat16)

    outs = pltpu.VMEM((p.blocks, p.ta, p.rg, p.tl, LANES), jnp.bfloat16)
    scratch = [
        pltpu.VMEM((p.blocks * p.nt, LANES), jnp.bfloat16),
        pltpu.VMEM((p.blocks * p.nt, p.rg * LANES), jnp.float32),
    ]
    return on_chip(body, [both, inner, outer], outs, scratch, (place,))


def cross(plan, jobs, owner, place, by_partner):
    p = plan
    scaling = 8.0 / (3.0 * SEG * NSEG)
    pair = 2 if p.rg % 2 == 0 else 1
    width = pair * LANES
    inputs, where = [], []
    for series, start, table in jobs:
        if not any(x is series[0] for x in inputs):
            inputs.extend(series)
        if not any(x is table for x in inputs):
            inputs.append(table)
        first = next(i for i, x in enumerate(inputs) if x is series[0])
        where.append((first, len(series), start, next(i for i, x in enumerate(inputs) if x is table)))

    def body(owner_ref, place_ref, *refs):
        outs, (spec, ref_spec) = refs[len(inputs) : -2], refs[-2:]
        turn = 0
        for q, (first, count, start, table) in enumerate(where):
            for r in range(0, p.rg, pair):
                slot = turn % 2
                turn += 1
                for n in range(p.blocks):
                    rows = []
                    for i in range(pair):
                        at = start + r + i
                        if count > 1:
                            x = [refs[first + m][n, at].astype(jnp.float32) for m in range(count)]
                            rows.append(jnp.concatenate(x, axis=0))
                        else:
                            rows.append(series_of(refs[first], n, at))
                    b = place_ref[1] ^ n if count > 1 and p.by_partner else n
                    spec[slot, b] = jnp.dot(
                        refs[table][...],
                        jnp.concatenate(rows, axis=1).astype(jnp.bfloat16),
                        preferred_element_type=jnp.float32,
                    )
                for s in range(NSEG):
                    at = s * ROWS
                    ref_spec[slot, at : at + ROWS, :] = spec[slot, owner_ref[s], at : at + ROWS, :]
                for n in range(p.blocks):
                    b = place_ref[1] ^ n if by_partner else n
                    co = jnp.zeros((8, width), jnp.float32)
                    quad = jnp.zeros((8, width), jnp.float32)
                    for s in range(NSEG):
                        at = s * ROWS
                        rc, rs = ref_spec[slot, at : at + 8, :], ref_spec[slot, at + 8 : at + 16, :]
                        qc, qs = spec[slot, b, at : at + 8, :], spec[slot, b, at + 8 : at + 16, :]
                        co = co + (rc * qc + rs * qs)
                        quad = quad + (rc * qs - rs * qc)
                    both = (jnp.concatenate([co, quad], axis=0) * scaling).astype(jnp.bfloat16)
                    for i in range(pair):
                        mine = both[:, i * LANES : (i + 1) * LANES]
                        if by_partner:
                            outs[n][q, r + i] = mine
                        else:
                            outs[0][n, q, r + i] = mine

    shape = (len(jobs), p.rg, ROWS, LANES)
    if by_partner:
        outs = [pltpu.VMEM(shape, jnp.bfloat16) for _ in range(p.blocks)]
    else:
        outs = [pltpu.VMEM((p.blocks,) + shape, jnp.bfloat16)]
    scratch = [
        pltpu.VMEM((2, p.blocks, NSEG * ROWS, width), jnp.float32),
        pltpu.VMEM((2, NSEG * ROWS, width), jnp.float32),
    ]
    return on_chip(body, inputs, outs, scratch, (owner, place))


def assemble(plan, so_far, quantities, pieces, place):
    p = plan
    shape = (4, 2, F, p.xb, p.cs)
    if not p.fast:
        if len(pieces) > 1:
            x = jnp.stack(pieces)
            x = jnp.take(x, jnp.arange(p.blocks, dtype=jnp.int32) ^ place[1], axis=0)
        else:
            x = pieces[0]
        out = jnp.zeros(shape, jnp.float32) if so_far is None else so_far
        x = x.reshape(p.blocks, len(quantities), p.rg, 2, 8, p.groups, p.cc)[:, :, :, :, :F]
        x = x.transpose(1, 3, 4, 5, 2, 0, 6).reshape((-1,) + shape[1:]).astype(jnp.float32)
        for n, quantity in enumerate(quantities):
            out = out.at[quantity].set(x[n])
        return out

    def body(place_ref, *refs):
        xs, swap = refs[: len(pieces)], refs[len(pieces)]
        out, by_chunk, wide, held, sems = refs[-5:]
        copies = []
        for n, quantity in enumerate(quantities):
            for j in range(p.blocks):
                if len(pieces) > 1:
                    by_chunk[place_ref[1] ^ j] = xs[j][n].reshape(p.rg * ROWS, LANES)
                else:
                    by_chunk[j] = xs[0][j, n].reshape(p.rg * ROWS, LANES)
            for tile in range(p.cs // LANES):
                lhs = [by_chunk[tile * p.groups + i] for i in range(p.groups)]
                swapped = jnp.dot(
                    jnp.concatenate(lhs, axis=1), swap[...], preferred_element_type=jnp.float32
                )
                for g in range(p.groups):
                    wide[tile, g] = swapped[:, g * LANES : (g + 1) * LANES]
            for part in range(2):
                for k in range(F):
                    for tile in range(p.cs // LANES):
                        for g in range(p.groups):
                            block = wide[tile, g, pl.ds(part * 8 + k, p.rg, stride=ROWS), :]
                            rows = slice(g * p.rg, (g + 1) * p.rg)
                            held[n, part, k, rows, tile * LANES : (tile + 1) * LANES] = block
                copies.append(
                    pltpu.make_async_copy(held.at[n, part], out.at[quantity, part], sems.at[n, part])
                )
                copies[-1].start()
        for copy in copies:
            copy.wait()

    before = [] if so_far is None else [so_far]
    scratch = [
        pltpu.VMEM((p.blocks, p.rg * ROWS, LANES), jnp.bfloat16),
        pltpu.VMEM((p.cs // LANES, p.groups, p.rg * ROWS, LANES), jnp.float32),
        pltpu.VMEM((len(quantities),) + shape[1:], jnp.float32),
        pltpu.SemaphoreType.DMA((len(quantities), 2)),
    ]
    return on_chip(
        body,
        [*pieces, group_swap(p)] + before,
        jax.ShapeDtypeStruct(shape, jnp.float32),
        scratch,
        (place,),
        in_hbm=len(before),
        **({"input_output_aliases": {len(pieces) + 2: 0}} if before else {}),
    )


def shards(velocity, offsets, owner):
    plan = Plan(velocity)
    block_axes = ("gx", "gz")
    time = lax.axis_index("ta").astype(jnp.int32)
    place = jnp.stack([time, lax.axis_index(block_axes).astype(jnp.int32)])

    both = pack_all(plan, velocity)
    both = both.reshape((-1,) + both.shape[2:])
    both = lax.all_to_all(both, block_axes + ("ta",), split_axis=0, concat_axis=0, tiled=True)
    both = both.reshape((plan.blocks, plan.ta) + both.shape[1:])

    def over_blocks(arrays):
        if len(arrays) == 1:
            return [lax.all_to_all(arrays[0], block_axes, split_axis=0, concat_axis=0, tiled=True)]
        return [arrays[0]] + [trade(arrays[n], block_axes, n, plan.blocks) for n in range(1, plan.blocks)]

    wall = pack_one(plan, velocity, 1, place)
    wall = over_blocks(wall)
    wall = regroup(plan, wall)
    wall = [wall[0]] + [trade(wall[m], "ta", m, plan.ta) for m in range(1, plan.ta)]

    times = jnp.arange(plan.tl, dtype=jnp.int32)[None, :]
    turn = jnp.arange(plan.ta, dtype=jnp.int32)[:, None]
    table_wall = dft_rows(offsets, ((turn ^ time) * plan.tl + times).reshape(-1))
    table = dft_rows(offsets, (turn * plan.tl + times).reshape(-1))
    early = cross(plan, [([both], 0, table), ([both], plan.rg, table)], owner, place, False)
    early = over_blocks(early)
    spin = vorticity(plan, both, place)
    late = cross(plan, [([spin], 0, table), (wall, 0, table_wall)], owner, place, plan.by_partner)
    late = over_blocks(late)
    out = assemble(plan, None, (2, 0), early, place)
    return assemble(plan, out, (3, 1), late, place)


def solution(mesh):
    in_specs = (P(None, "ta", "gx", "gz"), P(), P())
    out_specs = P(None, None, None, "gx", ("gz", "ta"))

    return jax.shard_map(shards, mesh=mesh, in_specs=in_specs, out_specs=out_specs, check_vma=False)
```

```python
import math

import jax
import jax.numpy as jnp
import numpy as np
from jax import lax
from jax.experimental import pallas as pl
from jax.experimental.pallas import tpu as pltpu
from jax.sharding import PartitionSpec as P

SEG = 16
NSEG = 7
F = 7
ROWS = 16
LANES = 128
PARTNERS = 8


class Plan:
    def __init__(self, velocity):
        _, self.tl, self.xb, self.zb = velocity.shape
        self.gx, self.gz, self.ta = (lax.axis_size(a) for a in ("gx", "gz", "ta"))
        self.blocks = self.gx * self.gz
        self.nt = self.tl * self.ta
        self.cs = self.zb // self.ta
        self.cc = self.cs // self.blocks
        self.groups = LANES // self.cc
        self.rg = self.xb // self.groups
        self.chunks = self.zb // self.cc
        assert self.groups * self.rg == self.xb and self.xb * 4 == LANES and self.cc >= 2
        assert self.ta & (self.ta - 1) == 0 and self.blocks & (self.blocks - 1) == 0
        self.by_partner = self.blocks <= PARTNERS
        self.fast = self.rg == 8 and self.tl == 8 and self.cs % LANES == 0


def on_chip(body, inputs, outs, scratch, scalars=(), in_hbm=0, **params):
    count = len(inputs) - in_hbm
    arrays = [pltpu.with_memory_space_constraint(x, pltpu.VMEM) for x in inputs[:count]]
    if not params:
        arrays += [pltpu.with_memory_space_constraint(x, pltpu.HBM) for x in inputs[count:]]
    else:
        arrays += inputs[count:]
    vmem = pl.BlockSpec(memory_space=pltpu.VMEM)
    smem = pl.BlockSpec(memory_space=pltpu.SMEM)
    hbm = pl.BlockSpec(memory_space=pl.ANY)
    return pl.pallas_call(
        body,
        in_specs=[smem] * len(scalars) + [vmem] * count + [hbm] * in_hbm,
        out_specs=jax.tree.map(lambda x: hbm if isinstance(x, jax.ShapeDtypeStruct) else vmem, outs),
        out_shape=outs,
        scratch_shapes=scratch,
        compiler_params=pltpu.CompilerParams(vmem_limit_bytes=24 << 20),
        **params,
    )(*scalars, *arrays)


def dft_rows(offsets, times):
    lag = times[None, :] - offsets[:, None]
    inside = (lag >= 0) & (lag < SEG)
    window = 0.5 - 0.5 * jnp.cos((2.0 * math.pi / SEG) * lag.astype(jnp.float32))
    frequency = jnp.arange(1, 9, dtype=jnp.int32)
    turns = (frequency[None, :, None] * lag[:, None, :]) % SEG
    angle = (2.0 * math.pi / SEG) * turns.astype(jnp.float32)
    keep = inside[:, None, :] & (frequency <= F)[None, :, None]
    weight = jnp.where(keep, window[:, None, :], jnp.float32(0.0))
    rows = jnp.stack([weight * jnp.cos(angle), -weight * jnp.sin(angle)], axis=1)
    return rows.reshape(offsets.shape[0] * ROWS, times.shape[0]).astype(jnp.bfloat16)


def trade(x, axis, step, count):
    return lax.ppermute(x, axis, [(i, i ^ step) for i in range(count)])


def group_swap(plan):
    p = plan
    size = p.groups * p.groups * p.cc
    at = np.arange(size).reshape(p.groups, p.groups, p.cc)
    matrix = np.zeros((size, size), np.float32)
    matrix[at.reshape(-1), at.transpose(1, 0, 2).reshape(-1)] = 1.0
    return jnp.asarray(matrix, jnp.bfloat16)


def side_picks(plan):
    p = plan
    matrix = np.zeros((p.rg, p.groups, p.cc, 2, p.groups, p.rg, 4), np.float32)
    for r in range(p.rg):
        for g in range(p.groups):
            for n in range(2):
                matrix[r, g, p.cc - 2 + n, 0, g, r, n] = 1.0
                matrix[r, g, n, 1, g, r, 2 + n] = 1.0
    return jnp.asarray(matrix.reshape(p.rg * LANES, 2 * LANES), jnp.bfloat16)


def spread_rows(plan, wide, tile, rows):
    p = plan
    rows = rows.astype(jnp.float32)
    for g in range(p.groups):
        wide[tile, g] = rows[:, g * p.rg : (g + 1) * p.rg].reshape(p.tl * p.rg, LANES)


def rows_by_snapshot(plan, wide, tiles):
    p = plan
    lhs = []
    for g in range(p.groups):
        rows = [wide[tile, g, pl.ds(r, p.tl, stride=p.rg), :] for tile in tiles for r in range(p.rg)]
        lhs.append(jnp.concatenate(rows, axis=0).astype(jnp.bfloat16))
    return jnp.concatenate(lhs, axis=1)


def pack_one(plan, velocity, quantity, packed, place):
    p = plan
    shape = (p.ta, p.rg + 1, p.tl, LANES)
    if not p.by_partner or not p.fast:
        x = velocity[quantity].reshape(p.tl, p.groups, p.rg, p.ta, p.blocks, p.cc)
        x = x.transpose(4, 3, 2, 0, 1, 5).reshape(p.blocks, p.ta, p.rg, p.tl, LANES)
        side = velocity[0].reshape(p.tl, p.xb, p.chunks, p.cc)
        before = jnp.roll(side[..., p.cc - 2 :], 1, axis=2)
        after = jnp.roll(side[..., :2], -1, axis=2)
        side = jnp.concatenate([before, after], axis=3).transpose(2, 0, 1, 3)
        side = side.reshape(p.ta, p.blocks, 1, p.tl, LANES).swapaxes(0, 1)
        x = jnp.concatenate([x, side], axis=2)
        x = jnp.take(x, jnp.arange(p.ta, dtype=jnp.int32) ^ place[0], axis=1)
        return [jnp.take(x, place[1] ^ n, axis=0) for n in range(p.blocks)] if p.by_partner else [x]
    per_slab = p.cs // LANES

    def body(place_ref, swap, picks, packed_ref, velocity_ref, *rest):
        outs = rest[: p.blocks]
        x, sems, wide, chunks = rest[p.blocks :]
        copies = []
        for m in range(p.ta):
            columns = pl.ds(pl.multiple_of((place_ref[0] ^ m) * p.cs, LANES), p.cs)
            copies.append(
                pltpu.make_async_copy(velocity_ref.at[quantity, :, :, columns], x.at[m], sems.at[m])
            )
            copies[-1].start()
        acc = jnp.zeros((p.chunks * p.tl, 2 * LANES), jnp.float32)
        for r in range(p.rg):
            rows = [
                packed_ref[c % p.blocks, c // p.blocks, p.rg + r].astype(jnp.float32)
                for c in range(p.chunks)
            ]
            acc = acc + jnp.dot(
                jnp.concatenate(rows, axis=0).astype(jnp.bfloat16),
                picks[r * LANES : (r + 1) * LANES, :],
                preferred_element_type=jnp.float32,
            )
        for c in range(p.chunks):
            before, after = (c + p.chunks - 1) % p.chunks, (c + 1) % p.chunks
            both = (
                acc[before * p.tl : (before + 1) * p.tl, :LANES]
                + acc[after * p.tl : (after + 1) * p.tl, LANES:]
            )
            chunks[c % p.blocks, place_ref[0] ^ (c // p.blocks), p.rg] = both.astype(jnp.bfloat16)
        for m in range(p.ta):
            copies[m].wait()
            for i in range(per_slab):
                spread_rows(p, wide, m * per_slab + i, x[m, :, :, i * LANES : (i + 1) * LANES])
        tiles = range(p.ta * per_slab)
        swapped = jnp.dot(
            rows_by_snapshot(p, wide, tiles), swap[...], preferred_element_type=jnp.float32
        ).astype(jnp.bfloat16)
        count = p.rg * p.tl
        for tile in tiles:
            m, i = divmod(tile, per_slab)
            for g in range(p.groups):
                mine = swapped[tile * count : (tile + 1) * count, g * LANES : (g + 1) * LANES]
                chunks[i * p.groups + g, m, 0 : p.rg] = mine.reshape(p.rg, p.tl, LANES)
        for n in range(p.blocks):
            outs[n][...] = chunks[place_ref[1] ^ n]

    outs = [pltpu.VMEM(shape, velocity.dtype) for _ in range(p.blocks)]
    scratch = [
        pltpu.VMEM((p.ta, p.tl, p.xb, p.cs), velocity.dtype),
        pltpu.SemaphoreType.DMA((p.ta,)),
        pltpu.VMEM((p.zb // LANES, p.groups, p.tl * p.rg, LANES), jnp.float32),
        pltpu.VMEM((p.blocks,) + shape, velocity.dtype),
    ]
    inputs = [group_swap(p), side_picks(p), packed, velocity]
    return on_chip(body, inputs, outs, scratch, (place,), in_hbm=1)


def regroup(plan, arrays):
    p = plan
    if len(arrays) == 1:
        return [arrays[0][:, m] for m in range(p.ta)]

    def body(*refs):
        for n in range(p.blocks):
            for m in range(p.ta):
                refs[p.blocks + m][n] = refs[n][m]

    outs = [pltpu.VMEM((p.blocks,) + arrays[0].shape[1:], arrays[0].dtype) for _ in range(p.ta)]
    return on_chip(body, list(arrays), outs, [])


def pack_all(plan, velocity):
    p = plan
    shape = (p.blocks, p.ta, 2 * p.rg, p.tl, LANES)
    if not p.fast:
        out = []
        for quantity in (2, 0):
            x = velocity[quantity].reshape(p.tl, p.groups, p.rg, p.ta, p.blocks, p.cc)
            out.append(x.transpose(4, 3, 2, 0, 1, 5).reshape(p.blocks, p.ta, p.rg, p.tl, LANES))
        return jnp.concatenate(out, axis=2)
    per_slab = p.cs // LANES
    half = max(p.ta // 2, 1)

    def body(swap_hbm, velocity_ref, out, x, sems, table_sems, wide, swap):
        table = pltpu.make_async_copy(swap_hbm, swap, table_sems.at[0])
        table.start()
        copies = {}
        for n, quantity in enumerate((2, 0)):
            for start in range(0, p.ta, half):
                columns = slice(start * p.cs, (start + half) * p.cs)
                copies[n, start] = pltpu.make_async_copy(
                    velocity_ref.at[quantity, :, :, columns], x.at[n, :, :, columns], sems.at[n, start]
                )
                copies[n, start].start()
        table.wait()
        count = p.rg * p.tl
        for n in range(2):
            for start in range(0, p.ta, half):
                copies[n, start].wait()
                tiles = range(start * per_slab, (start + half) * per_slab)
                for tile in tiles:
                    spread_rows(p, wide, tile, x[n, :, :, tile * LANES : (tile + 1) * LANES])
                swapped = jnp.dot(
                    rows_by_snapshot(p, wide, tiles), swap[...], preferred_element_type=jnp.float32
                )
                for tile in tiles:
                    at = (tile - tiles[0]) * count
                    m, i = divmod(tile, per_slab)
                    for g in range(p.groups):
                        mine = swapped[at : at + count, g * LANES : (g + 1) * LANES]
                        out[i * p.groups + g, m, n * p.rg : (n + 1) * p.rg] = mine.reshape(
                            p.rg, p.tl, LANES
                        ).astype(jnp.bfloat16)

    swap = group_swap(p)
    scratch = [
        pltpu.VMEM((2, p.tl, p.xb, p.zb), velocity.dtype),
        pltpu.SemaphoreType.DMA((2, p.ta)),
        pltpu.SemaphoreType.DMA((1,)),
        pltpu.VMEM((p.zb // LANES, p.groups, p.tl * p.rg, LANES), jnp.float32),
        pltpu.VMEM(swap.shape, swap.dtype),
    ]
    outs = pltpu.VMEM(shape, velocity.dtype)
    return on_chip(body, [swap, velocity], outs, scratch, in_hbm=2)


def slope_taps(plan):
    p = plan
    tap = {1: 8.0, -1: -8.0, 2: -1.0, -2: 1.0}
    inner = np.zeros((LANES, LANES), np.float32)
    outer = np.zeros((LANES, p.rg, LANES), np.float32)
    for g in range(p.groups):
        for c in range(p.cc):
            to = g * p.cc + c
            for ahead, weight in tap.items():
                at = c + ahead
                if 0 <= at < p.cc:
                    inner[g * p.cc + at, to] = weight
                else:
                    side = at + 2 if at < 0 else at - p.cc + 2
                    for r in range(p.rg):
                        outer[(g * p.rg + r) * 4 + side, r, to] = weight
    return jnp.asarray(inner, jnp.bfloat16), jnp.asarray(outer.reshape(LANES, -1), jnp.bfloat16)


def series_of(ref, b, r):
    x = [ref[b, m, r].astype(jnp.float32) for m in range(ref.shape[1])]
    return jnp.concatenate(x, axis=0)


def vorticity(plan, both, wall, place):
    p = plan
    inner, outer = slope_taps(p)

    def body(place_ref, x, inner_ref, outer_ref, *rest):
        arrived, (out, sides, slope, beside) = rest[: p.ta], rest[p.ta :]
        for m in range(p.ta):
            beside[m] = arrived[m][:, p.rg].astype(jnp.float32)

        def side_of(b):
            at = place_ref[1] ^ b if p.by_partner else b
            return jnp.concatenate([beside[place_ref[0] ^ t, at] for t in range(p.ta)], axis=0)

        chunk = place_ref[0] * p.blocks + place_ref[1]
        first = (chunk == 0).astype(jnp.int32)
        last = (chunk == p.chunks - 1).astype(jnp.int32)
        lane = lax.broadcasted_iota(jnp.int32, (p.nt, LANES), 1)
        for a in range(p.gx):
            for z in range(p.gz):
                before = a * p.gz + lax.rem(z + p.gz - first, p.gz)
                after = a * p.gz + lax.rem(z + last, p.gz)
                left, right = side_of(before), side_of(after)
                b = a * p.gz + z
                side = jnp.where(lane % 4 < 2, left, right).astype(jnp.bfloat16)
                sides[b * p.nt : (b + 1) * p.nt, :] = side
        slope[...] = jnp.dot(sides[...], outer_ref[...], preferred_element_type=jnp.float32)

        def row_of(a, z, r):
            shift, r = divmod(r, p.rg)
            own = series_of(x, (a % p.gx) * p.gz + z, r)
            if shift == 0:
                return own
            other = series_of(x, ((a + (1 if shift > 0 else -1)) % p.gx) * p.gz + z, r)
            width = shift * p.cc
            if shift > 0:
                return pltpu.roll(jnp.where(lane < width, other, own), LANES - width, 1)
            return pltpu.roll(jnp.where(lane >= LANES + width, other, own), -width, 1)

        for a in range(p.gx):
            for z in range(p.gz):
                b = a * p.gz + z
                rows = {r: row_of(a, z, r) for r in range(-2, p.rg + 2)}
                for r in range(p.rg):
                    across = 8.0 * (rows[r + 1] - rows[r - 1]) - (rows[r + 2] - rows[r - 2])
                    mine = series_of(x, b, p.rg + r).astype(jnp.bfloat16)
                    along = jnp.dot(mine, inner_ref[...], preferred_element_type=jnp.float32)
                    along = along + slope[b * p.nt : (b + 1) * p.nt, r * LANES : (r + 1) * LANES]
                    spin = (along - across) / 12.0
                    for m in range(p.ta):
                        out[b, m, r] = spin[m * p.tl : (m + 1) * p.tl].astype(jnp.bfloat16)

    outs = pltpu.VMEM((p.blocks, p.ta, p.rg, p.tl, LANES), jnp.bfloat16)
    scratch = [
        pltpu.VMEM((p.blocks * p.nt, LANES), jnp.bfloat16),
        pltpu.VMEM((p.blocks * p.nt, p.rg * LANES), jnp.float32),
        pltpu.VMEM((p.ta, p.blocks, p.tl, LANES), jnp.float32),
    ]
    return on_chip(body, [both, inner, outer, *wall], outs, scratch, (place,))


def cross(plan, jobs, owner, place, by_partner):
    p = plan
    scaling = 8.0 / (3.0 * SEG * NSEG)
    pair = 2 if p.rg % 2 == 0 else 1
    width = pair * LANES
    inputs, where = [], []
    for series, start, table in jobs:
        if not any(x is series[0] for x in inputs):
            inputs.extend(series)
        if not any(x is table for x in inputs):
            inputs.append(table)
        first = next(i for i, x in enumerate(inputs) if x is series[0])
        where.append((first, len(series), start, next(i for i, x in enumerate(inputs) if x is table)))

    def body(owner_ref, place_ref, *refs):
        outs, (spec, ref_spec) = refs[len(inputs) : -2], refs[-2:]
        turn = 0
        for q, (first, count, start, table) in enumerate(where):
            for r in range(0, p.rg, pair):
                slot = turn % 2
                turn += 1
                for n in range(p.blocks):
                    rows = []
                    for i in range(pair):
                        at = start + r + i
                        if count > 1:
                            x = [refs[first + m][n, at].astype(jnp.float32) for m in range(count)]
                            rows.append(jnp.concatenate(x, axis=0))
                        else:
                            rows.append(series_of(refs[first], n, at))
                    b = place_ref[1] ^ n if count > 1 and p.by_partner else n
                    spec[slot, b] = jnp.dot(
                        refs[table][...],
                        jnp.concatenate(rows, axis=1).astype(jnp.bfloat16),
                        preferred_element_type=jnp.float32,
                    )
                for s in range(NSEG):
                    at = s * ROWS
                    ref_spec[slot, at : at + ROWS, :] = spec[slot, owner_ref[s], at : at + ROWS, :]
                for n in range(p.blocks):
                    b = place_ref[1] ^ n if by_partner else n
                    co = jnp.zeros((8, width), jnp.float32)
                    quad = jnp.zeros((8, width), jnp.float32)
                    for s in range(NSEG):
                        at = s * ROWS
                        rc, rs = ref_spec[slot, at : at + 8, :], ref_spec[slot, at + 8 : at + 16, :]
                        qc, qs = spec[slot, b, at : at + 8, :], spec[slot, b, at + 8 : at + 16, :]
                        co = co + (rc * qc + rs * qs)
                        quad = quad + (rc * qs - rs * qc)
                    both = (jnp.concatenate([co, quad], axis=0) * scaling).astype(jnp.bfloat16)
                    for i in range(pair):
                        mine = both[:, i * LANES : (i + 1) * LANES]
                        if by_partner:
                            outs[n][q, r + i] = mine
                        else:
                            outs[0][n, q, r + i] = mine

    shape = (len(jobs), p.rg, ROWS, LANES)
    if by_partner:
        outs = [pltpu.VMEM(shape, jnp.bfloat16) for _ in range(p.blocks)]
    else:
        outs = [pltpu.VMEM((p.blocks,) + shape, jnp.bfloat16)]
    scratch = [
        pltpu.VMEM((2, p.blocks, NSEG * ROWS, width), jnp.float32),
        pltpu.VMEM((2, NSEG * ROWS, width), jnp.float32),
    ]
    return on_chip(body, inputs, outs, scratch, (owner, place))


def assemble(plan, so_far, quantities, pieces, place):
    p = plan
    shape = (4, 2, F, p.xb, p.cs)
    if not p.fast:
        if len(pieces) > 1:
            x = jnp.stack(pieces)
            x = jnp.take(x, jnp.arange(p.blocks, dtype=jnp.int32) ^ place[1], axis=0)
        else:
            x = pieces[0]
        out = jnp.zeros(shape, jnp.float32) if so_far is None else so_far
        x = x.reshape(p.blocks, len(quantities), p.rg, 2, 8, p.groups, p.cc)[:, :, :, :, :F]
        x = x.transpose(1, 3, 4, 5, 2, 0, 6).reshape((-1,) + shape[1:]).astype(jnp.float32)
        for n, quantity in enumerate(quantities):
            out = out.at[quantity].set(x[n])
        return out

    def body(place_ref, *refs):
        xs, swap = refs[: len(pieces)], refs[len(pieces)]
        out, by_chunk, wide, held, sems = refs[-5:]
        copies = []
        for n, quantity in enumerate(quantities):
            for j in range(p.blocks):
                if len(pieces) > 1:
                    by_chunk[place_ref[1] ^ j] = xs[j][n].reshape(p.rg * ROWS, LANES)
                else:
                    by_chunk[j] = xs[0][j, n].reshape(p.rg * ROWS, LANES)
            for tile in range(p.cs // LANES):
                lhs = [by_chunk[tile * p.groups + i] for i in range(p.groups)]
                swapped = jnp.dot(
                    jnp.concatenate(lhs, axis=1), swap[...], preferred_element_type=jnp.float32
                )
                for g in range(p.groups):
                    wide[tile, g] = swapped[:, g * LANES : (g + 1) * LANES]
            for part in range(2):
                for k in range(F):
                    for tile in range(p.cs // LANES):
                        for g in range(p.groups):
                            block = wide[tile, g, pl.ds(part * 8 + k, p.rg, stride=ROWS), :]
                            rows = slice(g * p.rg, (g + 1) * p.rg)
                            held[n, part, k, rows, tile * LANES : (tile + 1) * LANES] = block
                copies.append(
                    pltpu.make_async_copy(held.at[n, part], out.at[quantity, part], sems.at[n, part])
                )
                copies[-1].start()
        for copy in copies:
            copy.wait()

    before = [] if so_far is None else [so_far]
    scratch = [
        pltpu.VMEM((p.blocks, p.rg * ROWS, LANES), jnp.bfloat16),
        pltpu.VMEM((p.cs // LANES, p.groups, p.rg * ROWS, LANES), jnp.float32),
        pltpu.VMEM((len(quantities),) + shape[1:], jnp.float32),
        pltpu.SemaphoreType.DMA((len(quantities), 2)),
    ]
    return on_chip(
        body,
        [*pieces, group_swap(p)] + before,
        jax.ShapeDtypeStruct(shape, jnp.float32),
        scratch,
        (place,),
        in_hbm=len(before),
        **({"input_output_aliases": {len(pieces) + 2: 0}} if before else {}),
    )


def shards(velocity, offsets, owner):
    plan = Plan(velocity)
    block_axes = ("gx", "gz")
    time = lax.axis_index("ta").astype(jnp.int32)
    place = jnp.stack([time, lax.axis_index(block_axes).astype(jnp.int32)])

    packed = pack_all(plan, velocity)
    both = packed.reshape((-1,) + packed.shape[2:])
    both = lax.all_to_all(both, block_axes + ("ta",), split_axis=0, concat_axis=0, tiled=True)
    both = both.reshape((plan.blocks, plan.ta) + both.shape[1:])

    def over_blocks(arrays):
        if len(arrays) == 1:
            return [lax.all_to_all(arrays[0], block_axes, split_axis=0, concat_axis=0, tiled=True)]
        return [arrays[0]] + [trade(arrays[n], block_axes, n, plan.blocks) for n in range(1, plan.blocks)]

    wall = pack_one(plan, velocity, 1, packed, place)
    wall = over_blocks(wall)
    wall = regroup(plan, wall)
    wall = [wall[0]] + [trade(wall[m], "ta", m, plan.ta) for m in range(1, plan.ta)]

    times = jnp.arange(plan.tl, dtype=jnp.int32)[None, :]
    turn = jnp.arange(plan.ta, dtype=jnp.int32)[:, None]
    table_wall = dft_rows(offsets, ((turn ^ time) * plan.tl + times).reshape(-1))
    table = dft_rows(offsets, (turn * plan.tl + times).reshape(-1))
    early = cross(plan, [([both], 0, table), ([both], plan.rg, table)], owner, place, False)
    early = over_blocks(early)
    spin = vorticity(plan, both, wall, place)
    late = cross(plan, [([spin], 0, table), (wall, 0, table_wall)], owner, place, plan.by_partner)
    late = over_blocks(late)
    out = assemble(plan, None, (2, 0), early, place)
    return assemble(plan, out, (3, 1), late, place)


def solution(mesh):
    in_specs = (P(None, "ta", "gx", "gz"), P(), P())
    out_specs = P(None, None, None, "gx", ("gz", "ta"))

    return jax.shard_map(shards, mesh=mesh, in_specs=in_specs, out_specs=out_specs, check_vma=False)
```

```python
import math

import jax
import jax.numpy as jnp
import numpy as np
from jax import lax
from jax.experimental import pallas as pl
from jax.experimental.pallas import tpu as pltpu
from jax.sharding import PartitionSpec as P

SEG = 16
NSEG = 7
F = 7
ROWS = 16
LANES = 128
PARTNERS = 8


class Plan:
    def __init__(self, velocity):
        _, self.tl, self.xb, self.zb = velocity.shape
        self.gx, self.gz, self.ta = (lax.axis_size(a) for a in ("gx", "gz", "ta"))
        self.blocks = self.gx * self.gz
        self.nt = self.tl * self.ta
        self.cs = self.zb // self.ta
        self.cc = self.cs // self.blocks
        self.groups = LANES // self.cc
        self.rg = self.xb // self.groups
        self.chunks = self.zb // self.cc
        assert self.groups * self.rg == self.xb and self.xb * 4 == LANES and self.cc >= 2
        assert self.ta & (self.ta - 1) == 0 and self.blocks & (self.blocks - 1) == 0
        self.by_partner = self.blocks <= PARTNERS
        self.fast = self.rg == 8 and self.tl == 8 and self.cs % LANES == 0


def on_chip(body, inputs, outs, scratch, scalars=(), in_hbm=0, **params):
    count = len(inputs) - in_hbm
    arrays = [pltpu.with_memory_space_constraint(x, pltpu.VMEM) for x in inputs[:count]]
    if not params:
        arrays += [pltpu.with_memory_space_constraint(x, pltpu.HBM) for x in inputs[count:]]
    else:
        arrays += inputs[count:]
    vmem = pl.BlockSpec(memory_space=pltpu.VMEM)
    smem = pl.BlockSpec(memory_space=pltpu.SMEM)
    hbm = pl.BlockSpec(memory_space=pl.ANY)
    return pl.pallas_call(
        body,
        in_specs=[smem] * len(scalars) + [vmem] * count + [hbm] * in_hbm,
        out_specs=jax.tree.map(lambda x: hbm if isinstance(x, jax.ShapeDtypeStruct) else vmem, outs),
        out_shape=outs,
        scratch_shapes=scratch,
        compiler_params=pltpu.CompilerParams(vmem_limit_bytes=24 << 20),
        **params,
    )(*scalars, *arrays)


def dft_rows(offsets, times):
    lag = times[None, :] - offsets[:, None]
    inside = (lag >= 0) & (lag < SEG)
    window = 0.5 - 0.5 * jnp.cos((2.0 * math.pi / SEG) * lag.astype(jnp.float32))
    frequency = jnp.arange(1, 9, dtype=jnp.int32)
    turns = (frequency[None, :, None] * lag[:, None, :]) % SEG
    angle = (2.0 * math.pi / SEG) * turns.astype(jnp.float32)
    keep = inside[:, None, :] & (frequency <= F)[None, :, None]
    weight = jnp.where(keep, window[:, None, :], jnp.float32(0.0))
    rows = jnp.stack([weight * jnp.cos(angle), -weight * jnp.sin(angle)], axis=1)
    return rows.reshape(offsets.shape[0] * ROWS, times.shape[0]).astype(jnp.bfloat16)


def trade(x, axis, step, count):
    return lax.ppermute(x, axis, [(i, i ^ step) for i in range(count)])


def group_swap(plan):
    p = plan
    size = p.groups * p.groups * p.cc
    at = np.arange(size).reshape(p.groups, p.groups, p.cc)
    matrix = np.zeros((size, size), np.float32)
    matrix[at.reshape(-1), at.transpose(1, 0, 2).reshape(-1)] = 1.0
    return jnp.asarray(matrix, jnp.bfloat16)


def side_picks(plan):
    p = plan
    matrix = np.zeros((p.rg, p.groups, p.cc, 2, p.groups, p.rg, 4), np.float32)
    for r in range(p.rg):
        for g in range(p.groups):
            for n in range(2):
                matrix[r, g, p.cc - 2 + n, 0, g, r, n] = 1.0
                matrix[r, g, n, 1, g, r, 2 + n] = 1.0
    return jnp.asarray(matrix.reshape(p.rg * LANES, 2 * LANES), jnp.bfloat16)


def spread_rows(plan, wide, tile, rows):
    p = plan
    rows = rows.astype(jnp.float32)
    for g in range(p.groups):
        wide[tile, g] = rows[:, g * p.rg : (g + 1) * p.rg].reshape(p.tl * p.rg, LANES)


def rows_by_snapshot(plan, wide, tiles):
    p = plan
    lhs = []
    for g in range(p.groups):
        rows = [wide[tile, g, pl.ds(r, p.tl, stride=p.rg), :] for tile in tiles for r in range(p.rg)]
        lhs.append(jnp.concatenate(rows, axis=0).astype(jnp.bfloat16))
    return jnp.concatenate(lhs, axis=1)


def pack_one(plan, velocity, quantity, packed, place):
    p = plan
    shape = (p.ta, p.rg + 1, p.tl, LANES)
    if not p.by_partner or not p.fast:
        x = velocity[quantity].reshape(p.tl, p.groups, p.rg, p.ta, p.blocks, p.cc)
        x = x.transpose(4, 3, 2, 0, 1, 5).reshape(p.blocks, p.ta, p.rg, p.tl, LANES)
        side = velocity[0].reshape(p.tl, p.xb, p.chunks, p.cc)
        before = jnp.roll(side[..., p.cc - 2 :], 1, axis=2)
        after = jnp.roll(side[..., :2], -1, axis=2)
        side = jnp.concatenate([before, after], axis=3).transpose(2, 0, 1, 3)
        side = side.reshape(p.ta, p.blocks, 1, p.tl, LANES).swapaxes(0, 1)
        x = jnp.concatenate([x, side], axis=2)
        x = jnp.take(x, jnp.arange(p.ta, dtype=jnp.int32) ^ place[0], axis=1)
        return [jnp.take(x, place[1] ^ n, axis=0) for n in range(p.blocks)] if p.by_partner else [x]
    per_slab = p.cs // LANES

    def body(place_ref, swap, picks, packed_ref, velocity_ref, *rest):
        outs = rest[: p.blocks]
        x, sems, wide, chunks = rest[p.blocks :]
        copies = []
        for m in range(p.ta):
            columns = pl.ds(pl.multiple_of((place_ref[0] ^ m) * p.cs, LANES), p.cs)
            copies.append(
                pltpu.make_async_copy(velocity_ref.at[quantity, :, :, columns], x.at[m], sems.at[m])
            )
            copies[-1].start()
        acc = jnp.zeros((p.chunks * p.tl, 2 * LANES), jnp.float32)
        for r in range(p.rg):
            rows = [
                packed_ref[c % p.blocks, c // p.blocks, p.rg + r].astype(jnp.float32)
                for c in range(p.chunks)
            ]
            acc = acc + jnp.dot(
                jnp.concatenate(rows, axis=0).astype(jnp.bfloat16),
                picks[r * LANES : (r + 1) * LANES, :],
                preferred_element_type=jnp.float32,
            )
        for c in range(p.chunks):
            before, after = (c + p.chunks - 1) % p.chunks, (c + 1) % p.chunks
            both = (
                acc[before * p.tl : (before + 1) * p.tl, :LANES]
                + acc[after * p.tl : (after + 1) * p.tl, LANES:]
            )
            chunks[c % p.blocks, place_ref[0] ^ (c // p.blocks), p.rg] = both.astype(jnp.bfloat16)
        for m in range(p.ta):
            copies[m].wait()
            for i in range(per_slab):
                spread_rows(p, wide, m * per_slab + i, x[m, :, :, i * LANES : (i + 1) * LANES])
        tiles = range(p.ta * per_slab)
        swapped = jnp.dot(
            rows_by_snapshot(p, wide, tiles), swap[...], preferred_element_type=jnp.float32
        ).astype(jnp.bfloat16)
        count = p.rg * p.tl
        for tile in tiles:
            m, i = divmod(tile, per_slab)
            for g in range(p.groups):
                mine = swapped[tile * count : (tile + 1) * count, g * LANES : (g + 1) * LANES]
                chunks[i * p.groups + g, m, 0 : p.rg] = mine.reshape(p.rg, p.tl, LANES)
        for n in range(p.blocks):
            outs[n][...] = chunks[place_ref[1] ^ n]

    outs = [pltpu.VMEM(shape, velocity.dtype) for _ in range(p.blocks)]
    scratch = [
        pltpu.VMEM((p.ta, p.tl, p.xb, p.cs), velocity.dtype),
        pltpu.SemaphoreType.DMA((p.ta,)),
        pltpu.VMEM((p.zb // LANES, p.groups, p.tl * p.rg, LANES), jnp.float32),
        pltpu.VMEM((p.blocks,) + shape, velocity.dtype),
    ]
    inputs = [group_swap(p), side_picks(p), packed, velocity]
    return on_chip(body, inputs, outs, scratch, (place,), in_hbm=1)


def regroup(plan, arrays):
    p = plan
    if len(arrays) == 1:
        return [arrays[0][:, m] for m in range(p.ta)]

    def body(*refs):
        for n in range(p.blocks):
            for m in range(p.ta):
                refs[p.blocks + m][n] = refs[n][m]

    outs = [pltpu.VMEM((p.blocks,) + arrays[0].shape[1:], arrays[0].dtype) for _ in range(p.ta)]
    return on_chip(body, list(arrays), outs, [])


def pack_all(plan, velocity):
    p = plan
    shape = (p.blocks, p.ta, 2 * p.rg, p.tl, LANES)
    if not p.fast:
        out = []
        for quantity in (2, 0):
            x = velocity[quantity].reshape(p.tl, p.groups, p.rg, p.ta, p.blocks, p.cc)
            out.append(x.transpose(4, 3, 2, 0, 1, 5).reshape(p.blocks, p.ta, p.rg, p.tl, LANES))
        return jnp.concatenate(out, axis=2)
    per_slab = p.cs // LANES
    half = max(p.ta // 2, 1)

    def body(swap_hbm, velocity_ref, out, x, sems, table_sems, wide, swap):
        table = pltpu.make_async_copy(swap_hbm, swap, table_sems.at[0])
        table.start()
        copies = {}
        for n, quantity in enumerate((2, 0)):
            for start in range(0, p.ta, half):
                columns = slice(start * p.cs, (start + half) * p.cs)
                copies[n, start] = pltpu.make_async_copy(
                    velocity_ref.at[quantity, :, :, columns], x.at[n, :, :, columns], sems.at[n, start]
                )
                copies[n, start].start()
        table.wait()
        count = p.rg * p.tl
        for n in range(2):
            for start in range(0, p.ta, half):
                copies[n, start].wait()
                tiles = range(start * per_slab, (start + half) * per_slab)
                for tile in tiles:
                    spread_rows(p, wide, tile, x[n, :, :, tile * LANES : (tile + 1) * LANES])
                swapped = jnp.dot(
                    rows_by_snapshot(p, wide, tiles), swap[...], preferred_element_type=jnp.float32
                )
                for tile in tiles:
                    at = (tile - tiles[0]) * count
                    m, i = divmod(tile, per_slab)
                    for g in range(p.groups):
                        mine = swapped[at : at + count, g * LANES : (g + 1) * LANES]
                        out[i * p.groups + g, m, n * p.rg : (n + 1) * p.rg] = mine.reshape(
                            p.rg, p.tl, LANES
                        ).astype(jnp.bfloat16)

    swap = group_swap(p)
    scratch = [
        pltpu.VMEM((2, p.tl, p.xb, p.zb), velocity.dtype),
        pltpu.SemaphoreType.DMA((2, p.ta)),
        pltpu.SemaphoreType.DMA((1,)),
        pltpu.VMEM((p.zb // LANES, p.groups, p.tl * p.rg, LANES), jnp.float32),
        pltpu.VMEM(swap.shape, swap.dtype),
    ]
    outs = pltpu.VMEM(shape, velocity.dtype)
    return on_chip(body, [swap, velocity], outs, scratch, in_hbm=2)


def slope_taps(plan):
    p = plan
    tap = {1: 8.0, -1: -8.0, 2: -1.0, -2: 1.0}
    inner = np.zeros((LANES, LANES), np.float32)
    outer = np.zeros((LANES, p.rg, LANES), np.float32)
    for g in range(p.groups):
        for c in range(p.cc):
            to = g * p.cc + c
            for ahead, weight in tap.items():
                at = c + ahead
                if 0 <= at < p.cc:
                    inner[g * p.cc + at, to] = weight
                else:
                    side = at + 2 if at < 0 else at - p.cc + 2
                    for r in range(p.rg):
                        outer[(g * p.rg + r) * 4 + side, r, to] = weight
    return jnp.asarray(inner, jnp.bfloat16), jnp.asarray(outer.reshape(LANES, -1), jnp.bfloat16)


def series_of(ref, b, r):
    x = [ref[b, m, r].astype(jnp.float32) for m in range(ref.shape[1])]
    return jnp.concatenate(x, axis=0)


def inner_vorticity(plan, both):
    p = plan
    inner, _ = slope_taps(p)

    def body(x, inner_ref, out):
        lane = lax.broadcasted_iota(jnp.int32, (p.nt, LANES), 1)

        def row_of(a, z, r):
            shift, r = divmod(r, p.rg)
            own = series_of(x, (a % p.gx) * p.gz + z, r)
            if shift == 0:
                return own
            other = series_of(x, ((a + (1 if shift > 0 else -1)) % p.gx) * p.gz + z, r)
            width = shift * p.cc
            if shift > 0:
                return pltpu.roll(jnp.where(lane < width, other, own), LANES - width, 1)
            return pltpu.roll(jnp.where(lane >= LANES + width, other, own), -width, 1)

        for a in range(p.gx):
            for z in range(p.gz):
                b = a * p.gz + z
                rows = {r: row_of(a, z, r) for r in range(-2, p.rg + 2)}
                for r in range(p.rg):
                    across = 8.0 * (rows[r + 1] - rows[r - 1]) - (rows[r + 2] - rows[r - 2])
                    mine = series_of(x, b, p.rg + r).astype(jnp.bfloat16)
                    along = jnp.dot(mine, inner_ref[...], preferred_element_type=jnp.float32)
                    out[b, r] = along - across

    outs = pltpu.VMEM((p.blocks, p.rg, p.nt, LANES), jnp.float32)
    return on_chip(body, [both, inner], outs, [])


def cross_spin_and(plan, base, wall, table, table_wall, owner, place, by_partner):
    p = plan
    _, outer = slope_taps(p)

    def prepare(place_ref, outer_ref, arrived, sides, slope, beside):
        chunk = place_ref[0] * p.blocks + place_ref[1]
        first = (chunk == 0).astype(jnp.int32)
        last = (chunk == p.chunks - 1).astype(jnp.int32)
        is_left = (lax.broadcasted_iota(jnp.int32, (p.nt, LANES), 1) & 3) < 2
        for m in range(p.ta):
            beside[m] = arrived[m][:, p.rg].astype(jnp.float32)

        def side_of(b):
            at = place_ref[1] ^ b if p.by_partner else b
            return jnp.concatenate([beside[place_ref[0] ^ t, at] for t in range(p.ta)], axis=0)

        for a in range(p.gx):
            for z in range(p.gz):
                before = a * p.gz + lax.rem(z + p.gz - first, p.gz)
                after = a * p.gz + lax.rem(z + last, p.gz)
                b = a * p.gz + z
                side = jnp.where(is_left, side_of(before), side_of(after))
                sides[b * p.nt : (b + 1) * p.nt, :] = side.astype(jnp.bfloat16)
        slope[...] = jnp.dot(sides[...], outer_ref[...], preferred_element_type=jnp.float32)

    scratch = [
        pltpu.VMEM((p.blocks * p.nt, LANES), jnp.bfloat16),
        pltpu.VMEM((p.blocks * p.nt, p.rg * LANES), jnp.float32),
        pltpu.VMEM((p.ta, p.blocks, p.tl, LANES), jnp.float32),
    ]
    jobs = [(wall, 0, table_wall), ([base], 0, table)]
    return cross(plan, jobs, owner, place, by_partner, (outer, prepare, scratch))


def cross(plan, jobs, owner, place, by_partner, spin=None):
    p = plan
    scaling = 8.0 / (3.0 * SEG * NSEG)
    pair = 2 if p.rg % 2 == 0 else 1
    width = pair * LANES
    inputs, where = [], []
    for series, start, table in jobs:
        if not any(x is series[0] for x in inputs):
            inputs.extend(series)
        if not any(x is table for x in inputs):
            inputs.append(table)
        first = next(i for i, x in enumerate(inputs) if x is series[0])
        where.append((first, len(series), start, next(i for i, x in enumerate(inputs) if x is table)))

    if spin is not None:
        outer, prepare, more_scratch = spin
        inputs.append(outer)

    def body(owner_ref, place_ref, *refs):
        outs = refs[len(inputs) : len(inputs) + n_outs]
        if by_partner:
            spec_0, spec_1, ref_0, ref_1 = refs[len(inputs) + n_outs :][:4]
            turns = ((spec_0, ref_0), (spec_1, ref_1))
        else:
            specs, ref_specs = refs[len(inputs) + n_outs :][:2]
            turns = tuple((specs.at[i], ref_specs.at[i]) for i in range(2))
        more = refs[len(refs) - 3 :]
        turn = 0
        for q, (first, count, start, table) in enumerate(where):
            whole = inputs[first].dtype == jnp.float32
            if whole:
                arrived = refs[where[0][0] : where[0][0] + where[0][1]]
                prepare(place_ref, refs[len(inputs) - 1], arrived, *more)
            for r in range(0, p.rg, pair):
                spec, ref_spec = turns[turn % 2]
                turn += 1
                for n in range(p.blocks):
                    rows = []
                    for i in range(pair):
                        at = start + r + i
                        if whole:
                            slope = more[1][n * p.nt : (n + 1) * p.nt, at * LANES : (at + 1) * LANES]
                            rows.append((refs[first][n, at] + slope) / 12.0)
                        elif count > 1:
                            x = [refs[first + m][n, at].astype(jnp.float32) for m in range(count)]
                            rows.append(jnp.concatenate(x, axis=0))
                        else:
                            rows.append(series_of(refs[first], n, at))
                    b = place_ref[1] ^ n if count > 1 and p.by_partner else n
                    spec[b] = jnp.dot(
                        refs[table][...],
                        jnp.concatenate(rows, axis=1).astype(jnp.bfloat16),
                        preferred_element_type=jnp.float32,
                    )
                for s in range(NSEG):
                    at = s * ROWS
                    ref_spec[at : at + ROWS, :] = spec[owner_ref[s], at : at + ROWS, :]
                for n in range(p.blocks):
                    b = place_ref[1] ^ n if by_partner else n
                    co = jnp.zeros((8, width), jnp.float32)
                    quad = jnp.zeros((8, width), jnp.float32)
                    for s in range(NSEG):
                        at = s * ROWS
                        rc, rs = ref_spec[at : at + 8, :], ref_spec[at + 8 : at + 16, :]
                        qc, qs = spec[b, at : at + 8, :], spec[b, at + 8 : at + 16, :]
                        co = co + (rc * qc + rs * qs)
                        quad = quad + (rc * qs - rs * qc)
                    both = (jnp.concatenate([co, quad], axis=0) * scaling).astype(jnp.bfloat16)
                    for i in range(pair):
                        mine = both[:, i * LANES : (i + 1) * LANES]
                        if by_partner:
                            outs[n][q, r + i] = mine
                        else:
                            outs[0][n, q, r + i] = mine

    shape = (len(jobs), p.rg, ROWS, LANES)
    if by_partner:
        outs = [pltpu.VMEM(shape, jnp.bfloat16) for _ in range(p.blocks)]
    else:
        outs = [pltpu.VMEM((p.blocks,) + shape, jnp.bfloat16)]
    n_outs = len(outs)
    spec_shape, ref_shape = (p.blocks, NSEG * ROWS, width), (NSEG * ROWS, width)
    if by_partner:
        scratch = [pltpu.VMEM(x, jnp.float32) for x in (spec_shape, spec_shape, ref_shape, ref_shape)]
    else:
        scratch = [pltpu.VMEM((2,) + x, jnp.float32) for x in (spec_shape, ref_shape)]
    scratch += more_scratch if spin is not None else []
    return on_chip(body, inputs, outs, scratch, (owner, place))


def assemble(plan, so_far, quantities, pieces, place):
    p = plan
    shape = (4, 2, F, p.xb, p.cs)
    if not p.fast:
        if len(pieces) > 1:
            x = jnp.stack(pieces)
            x = jnp.take(x, jnp.arange(p.blocks, dtype=jnp.int32) ^ place[1], axis=0)
        else:
            x = pieces[0]
        out = jnp.zeros(shape, jnp.float32) if so_far is None else so_far
        x = x.reshape(p.blocks, len(quantities), p.rg, 2, 8, p.groups, p.cc)[:, :, :, :, :F]
        x = x.transpose(1, 3, 4, 5, 2, 0, 6).reshape((-1,) + shape[1:]).astype(jnp.float32)
        for n, quantity in enumerate(quantities):
            out = out.at[quantity].set(x[n])
        return out

    def body(place_ref, *refs):
        xs, swap = refs[: len(pieces)], refs[len(pieces)]
        out, by_chunk, wide, held, sems = refs[-5:]
        copies = []
        for n, quantity in enumerate(quantities):
            for j in range(p.blocks):
                if len(pieces) > 1:
                    by_chunk[place_ref[1] ^ j] = xs[j][n].reshape(p.rg * ROWS, LANES)
                else:
                    by_chunk[j] = xs[0][j, n].reshape(p.rg * ROWS, LANES)
            for tile in range(p.cs // LANES):
                lhs = [by_chunk[tile * p.groups + i] for i in range(p.groups)]
                swapped = jnp.dot(
                    jnp.concatenate(lhs, axis=1), swap[...], preferred_element_type=jnp.float32
                )
                for g in range(p.groups):
                    wide[tile, g] = swapped[:, g * LANES : (g + 1) * LANES]
            for part in range(2):
                for k in range(F):
                    for tile in range(p.cs // LANES):
                        for g in range(p.groups):
                            block = wide[tile, g, pl.ds(part * 8 + k, p.rg, stride=ROWS), :]
                            rows = slice(g * p.rg, (g + 1) * p.rg)
                            held[n, part, k, rows, tile * LANES : (tile + 1) * LANES] = block
                copies.append(
                    pltpu.make_async_copy(held.at[n, part], out.at[quantity, part], sems.at[n, part])
                )
                copies[-1].start()
        for copy in copies:
            copy.wait()

    before = [] if so_far is None else [so_far]
    scratch = [
        pltpu.VMEM((p.blocks, p.rg * ROWS, LANES), jnp.bfloat16),
        pltpu.VMEM((p.cs // LANES, p.groups, p.rg * ROWS, LANES), jnp.float32),
        pltpu.VMEM((len(quantities),) + shape[1:], jnp.float32),
        pltpu.SemaphoreType.DMA((len(quantities), 2)),
    ]
    return on_chip(
        body,
        [*pieces, group_swap(p)] + before,
        jax.ShapeDtypeStruct(shape, jnp.float32),
        scratch,
        (place,),
        in_hbm=len(before),
        **({"input_output_aliases": {len(pieces) + 2: 0}} if before else {}),
    )


def shards(velocity, offsets, owner):
    plan = Plan(velocity)
    block_axes = ("gx", "gz")
    time = lax.axis_index("ta").astype(jnp.int32)
    place = jnp.stack([time, lax.axis_index(block_axes).astype(jnp.int32)])

    packed = pack_all(plan, velocity)
    both = packed.reshape((-1,) + packed.shape[2:])
    both = lax.all_to_all(both, block_axes + ("ta",), split_axis=0, concat_axis=0, tiled=True)
    both = both.reshape((plan.blocks, plan.ta) + both.shape[1:])

    def over_blocks(arrays):
        if len(arrays) == 1:
            return [lax.all_to_all(arrays[0], block_axes, split_axis=0, concat_axis=0, tiled=True)]
        traded = {n: trade(arrays[n], block_axes, n, plan.blocks) for n in range(1, plan.blocks)}
        return [arrays[0]] + [traded[n] for n in range(1, plan.blocks)]

    wall = pack_one(plan, velocity, 1, packed, place)
    wall = over_blocks(wall)
    wall = regroup(plan, wall)
    wall = [wall[0]] + [trade(wall[m], "ta", m, plan.ta) for m in range(1, plan.ta)]

    times = jnp.arange(plan.tl, dtype=jnp.int32)[None, :]
    turn = jnp.arange(plan.ta, dtype=jnp.int32)[:, None]
    table_wall = dft_rows(offsets, ((turn ^ time) * plan.tl + times).reshape(-1))
    table = dft_rows(offsets, (turn * plan.tl + times).reshape(-1))
    early = cross(plan, [([both], 0, table), ([both], plan.rg, table)], owner, place, False)
    early = over_blocks(early)
    base = inner_vorticity(plan, both)
    late = cross_spin_and(plan, base, wall, table, table_wall, owner, place, plan.by_partner)
    late = over_blocks(late)
    out = assemble(plan, None, (2, 0), early, place)
    return assemble(plan, out, (1, 3), late, place)


def solution(mesh):
    in_specs = (P(None, "ta", "gx", "gz"), P(), P())
    out_specs = P(None, None, None, "gx", ("gz", "ta"))

    return jax.shard_map(shards, mesh=mesh, in_specs=in_specs, out_specs=out_specs, check_vma=False)
```

```python
import math

import jax
import jax.numpy as jnp
import numpy as np
from jax import lax
from jax.experimental import pallas as pl
from jax.experimental.pallas import tpu as pltpu
from jax.sharding import PartitionSpec as P

SEG = 16
NSEG = 7
F = 7
ROWS = 16
LANES = 128
PARTNERS = 8


class Plan:
    def __init__(self, velocity):
        _, self.tl, self.xb, self.zb = velocity.shape
        self.gx, self.gz, self.ta = (lax.axis_size(a) for a in ("gx", "gz", "ta"))
        self.blocks = self.gx * self.gz
        self.nt = self.tl * self.ta
        self.cs = self.zb // self.ta
        self.cc = self.cs // self.blocks
        self.groups = LANES // self.cc
        self.rg = self.xb // self.groups
        self.chunks = self.zb // self.cc
        assert self.groups * self.rg == self.xb and self.xb * 4 == LANES and self.cc >= 2
        assert self.ta & (self.ta - 1) == 0 and self.blocks & (self.blocks - 1) == 0
        self.by_partner = self.blocks <= PARTNERS
        self.fast = self.rg == 8 and self.tl == 8 and self.cs % LANES == 0


def on_chip(body, inputs, outs, scratch, scalars=(), in_hbm=0, **params):
    count = len(inputs) - in_hbm
    arrays = [pltpu.with_memory_space_constraint(x, pltpu.VMEM) for x in inputs[:count]]
    if not params:
        arrays += [pltpu.with_memory_space_constraint(x, pltpu.HBM) for x in inputs[count:]]
    else:
        arrays += inputs[count:]
    vmem = pl.BlockSpec(memory_space=pltpu.VMEM)
    smem = pl.BlockSpec(memory_space=pltpu.SMEM)
    hbm = pl.BlockSpec(memory_space=pl.ANY)
    return pl.pallas_call(
        body,
        in_specs=[smem] * len(scalars) + [vmem] * count + [hbm] * in_hbm,
        out_specs=jax.tree.map(lambda x: hbm if isinstance(x, jax.ShapeDtypeStruct) else vmem, outs),
        out_shape=outs,
        scratch_shapes=scratch,
        compiler_params=pltpu.CompilerParams(vmem_limit_bytes=24 << 20),
        **params,
    )(*scalars, *arrays)


def dft_rows(offsets, times):
    lag = times[None, :] - offsets[:, None]
    inside = (lag >= 0) & (lag < SEG)
    window = 0.5 - 0.5 * jnp.cos((2.0 * math.pi / SEG) * lag.astype(jnp.float32))
    frequency = jnp.arange(1, 9, dtype=jnp.int32)
    turns = (frequency[None, :, None] * lag[:, None, :]) % SEG
    angle = (2.0 * math.pi / SEG) * turns.astype(jnp.float32)
    keep = inside[:, None, :] & (frequency <= F)[None, :, None]
    weight = jnp.where(keep, window[:, None, :], jnp.float32(0.0))
    rows = jnp.stack([weight * jnp.cos(angle), -weight * jnp.sin(angle)], axis=1)
    return rows.reshape(offsets.shape[0] * ROWS, times.shape[0]).astype(jnp.bfloat16)


def trade(x, axis, step, count):
    return lax.ppermute(x, axis, [(i, i ^ step) for i in range(count)])


def group_swap(plan):
    p = plan
    size = p.groups * p.groups * p.cc
    at = np.arange(size).reshape(p.groups, p.groups, p.cc)
    matrix = np.zeros((size, size), np.float32)
    matrix[at.reshape(-1), at.transpose(1, 0, 2).reshape(-1)] = 1.0
    return jnp.asarray(matrix, jnp.bfloat16)


def side_picks(plan):
    p = plan
    matrix = np.zeros((p.rg, p.groups, p.cc, 2, p.groups, p.rg, 4), np.float32)
    for r in range(p.rg):
        for g in range(p.groups):
            for n in range(2):
                matrix[r, g, p.cc - 2 + n, 0, g, r, n] = 1.0
                matrix[r, g, n, 1, g, r, 2 + n] = 1.0
    return jnp.asarray(matrix.reshape(p.rg * LANES, 2 * LANES), jnp.bfloat16)


def spread_rows(plan, wide, tile, rows):
    p = plan
    rows = rows.astype(jnp.float32)
    for g in range(p.groups):
        wide[tile, g] = rows[:, g * p.rg : (g + 1) * p.rg].reshape(p.tl * p.rg, LANES)


def rows_by_snapshot(plan, wide, tiles):
    p = plan
    lhs = []
    for g in range(p.groups):
        rows = [wide[tile, g, pl.ds(r, p.tl, stride=p.rg), :] for tile in tiles for r in range(p.rg)]
        lhs.append(jnp.concatenate(rows, axis=0).astype(jnp.bfloat16))
    return jnp.concatenate(lhs, axis=1)


def pack_one(plan, velocity, quantity, packed, place):
    p = plan
    shape = (p.ta, p.rg + 1, p.tl, LANES)
    if not p.by_partner or not p.fast:
        x = velocity[quantity].reshape(p.tl, p.groups, p.rg, p.ta, p.blocks, p.cc)
        x = x.transpose(4, 3, 2, 0, 1, 5).reshape(p.blocks, p.ta, p.rg, p.tl, LANES)
        side = velocity[0].reshape(p.tl, p.xb, p.chunks, p.cc)
        before = jnp.roll(side[..., p.cc - 2 :], 1, axis=2)
        after = jnp.roll(side[..., :2], -1, axis=2)
        side = jnp.concatenate([before, after], axis=3).transpose(2, 0, 1, 3)
        side = side.reshape(p.ta, p.blocks, 1, p.tl, LANES).swapaxes(0, 1)
        x = jnp.concatenate([x, side], axis=2)
        x = jnp.take(x, jnp.arange(p.ta, dtype=jnp.int32) ^ place[0], axis=1)
        return [jnp.take(x, place[1] ^ n, axis=0) for n in range(p.blocks)] if p.by_partner else [x]
    per_slab = p.cs // LANES

    def body(place_ref, swap, picks, packed_ref, velocity_ref, *rest):
        outs = rest[: p.blocks]
        x, sems, wide, chunks = rest[p.blocks :]
        copies = []
        for m in range(p.ta):
            columns = pl.ds(pl.multiple_of((place_ref[0] ^ m) * p.cs, LANES), p.cs)
            copies.append(
                pltpu.make_async_copy(velocity_ref.at[quantity, :, :, columns], x.at[m], sems.at[m])
            )
            copies[-1].start()
        acc = jnp.zeros((p.chunks * p.tl, 2 * LANES), jnp.float32)
        for r in range(p.rg):
            rows = [
                packed_ref[c % p.blocks, c // p.blocks, p.rg + r].astype(jnp.float32)
                for c in range(p.chunks)
            ]
            acc = acc + jnp.dot(
                jnp.concatenate(rows, axis=0).astype(jnp.bfloat16),
                picks[r * LANES : (r + 1) * LANES, :],
                preferred_element_type=jnp.float32,
            )
        for c in range(p.chunks):
            before, after = (c + p.chunks - 1) % p.chunks, (c + 1) % p.chunks
            both = (
                acc[before * p.tl : (before + 1) * p.tl, :LANES]
                + acc[after * p.tl : (after + 1) * p.tl, LANES:]
            )
            chunks[c % p.blocks, place_ref[0] ^ (c // p.blocks), p.rg] = both.astype(jnp.bfloat16)
        for m in range(p.ta):
            copies[m].wait()
            for i in range(per_slab):
                spread_rows(p, wide, m * per_slab + i, x[m, :, :, i * LANES : (i + 1) * LANES])
        tiles = range(p.ta * per_slab)
        swapped = jnp.dot(
            rows_by_snapshot(p, wide, tiles), swap[...], preferred_element_type=jnp.float32
        ).astype(jnp.bfloat16)
        count = p.rg * p.tl
        for tile in tiles:
            m, i = divmod(tile, per_slab)
            for g in range(p.groups):
                mine = swapped[tile * count : (tile + 1) * count, g * LANES : (g + 1) * LANES]
                chunks[i * p.groups + g, m, 0 : p.rg] = mine.reshape(p.rg, p.tl, LANES)
        for n in range(p.blocks):
            outs[n][...] = chunks[place_ref[1] ^ n]

    outs = [pltpu.VMEM(shape, velocity.dtype) for _ in range(p.blocks)]
    scratch = [
        pltpu.VMEM((p.ta, p.tl, p.xb, p.cs), velocity.dtype),
        pltpu.SemaphoreType.DMA((p.ta,)),
        pltpu.VMEM((p.zb // LANES, p.groups, p.tl * p.rg, LANES), jnp.float32),
        pltpu.VMEM((p.blocks,) + shape, velocity.dtype),
    ]
    inputs = [group_swap(p), side_picks(p), packed, velocity]
    return on_chip(body, inputs, outs, scratch, (place,), in_hbm=1)


def regroup(plan, arrays):
    p = plan
    if len(arrays) == 1:
        return [arrays[0][:, m] for m in range(p.ta)]

    def body(*refs):
        for n in range(p.blocks):
            for m in range(p.ta):
                refs[p.blocks + m][n] = refs[n][m]

    outs = [pltpu.VMEM((p.blocks,) + arrays[0].shape[1:], arrays[0].dtype) for _ in range(p.ta)]
    return on_chip(body, list(arrays), outs, [])


def pack_all(plan, velocity):
    p = plan
    shape = (p.blocks, p.ta, 2 * p.rg, p.tl, LANES)
    if not p.fast:
        out = []
        for quantity in (2, 0):
            x = velocity[quantity].reshape(p.tl, p.groups, p.rg, p.ta, p.blocks, p.cc)
            out.append(x.transpose(4, 3, 2, 0, 1, 5).reshape(p.blocks, p.ta, p.rg, p.tl, LANES))
        return jnp.concatenate(out, axis=2)
    per_slab = p.cs // LANES

    def body(swap_hbm, velocity_ref, out, x, sems, table_sems, wide, swap):
        table = pltpu.make_async_copy(swap_hbm, swap, table_sems.at[0])
        copies = []
        for n, quantity in enumerate((2, 0)):
            copies.append(pltpu.make_async_copy(velocity_ref.at[quantity], x.at[n], sems.at[n]))
            copies[-1].start()
            if n == 0:
                table.start()
        table.wait()
        count = p.rg * p.tl
        tiles = range(p.zb // LANES)
        for n in range(2):
            copies[n].wait()
            for tile in tiles:
                spread_rows(p, wide, tile, x[n, :, :, tile * LANES : (tile + 1) * LANES])
            swapped = jnp.dot(
                rows_by_snapshot(p, wide, tiles), swap[...], preferred_element_type=jnp.float32
            )
            for tile in tiles:
                m, i = divmod(tile, per_slab)
                for g in range(p.groups):
                    mine = swapped[tile * count : (tile + 1) * count, g * LANES : (g + 1) * LANES]
                    out[i * p.groups + g, m, n * p.rg : (n + 1) * p.rg] = mine.reshape(
                        p.rg, p.tl, LANES
                    ).astype(jnp.bfloat16)

    swap = group_swap(p)
    scratch = [
        pltpu.VMEM((2, p.tl, p.xb, p.zb), velocity.dtype),
        pltpu.SemaphoreType.DMA((2,)),
        pltpu.SemaphoreType.DMA((1,)),
        pltpu.VMEM((p.zb // LANES, p.groups, p.tl * p.rg, LANES), jnp.float32),
        pltpu.VMEM(swap.shape, swap.dtype),
    ]
    outs = pltpu.VMEM(shape, velocity.dtype)
    return on_chip(body, [swap, velocity], outs, scratch, in_hbm=2)


def slope_taps(plan):
    p = plan
    tap = {1: 8.0, -1: -8.0, 2: -1.0, -2: 1.0}
    inner = np.zeros((LANES, LANES), np.float32)
    outer = np.zeros((LANES, p.rg, LANES), np.float32)
    for g in range(p.groups):
        for c in range(p.cc):
            to = g * p.cc + c
            for ahead, weight in tap.items():
                at = c + ahead
                if 0 <= at < p.cc:
                    inner[g * p.cc + at, to] = weight
                else:
                    side = at + 2 if at < 0 else at - p.cc + 2
                    for r in range(p.rg):
                        outer[(g * p.rg + r) * 4 + side, r, to] = weight
    return jnp.asarray(inner, jnp.bfloat16), jnp.asarray(outer.reshape(LANES, -1), jnp.bfloat16)


def series_of(ref, b, r):
    x = [ref[b, m, r].astype(jnp.float32) for m in range(ref.shape[1])]
    return jnp.concatenate(x, axis=0)


def inner_vorticity(plan, both):
    p = plan
    inner, _ = slope_taps(p)

    def body(x, inner_ref, out):
        lane = lax.broadcasted_iota(jnp.int32, (p.nt, LANES), 1)

        def row_of(a, z, r):
            shift, r = divmod(r, p.rg)
            own = series_of(x, (a % p.gx) * p.gz + z, r)
            if shift == 0:
                return own
            other = series_of(x, ((a + (1 if shift > 0 else -1)) % p.gx) * p.gz + z, r)
            width = shift * p.cc
            if shift > 0:
                return pltpu.roll(jnp.where(lane < width, other, own), LANES - width, 1)
            return pltpu.roll(jnp.where(lane >= LANES + width, other, own), -width, 1)

        for a in range(p.gx):
            for z in range(p.gz):
                b = a * p.gz + z
                rows = {r: row_of(a, z, r) for r in range(-2, p.rg + 2)}
                for r in range(p.rg):
                    across = 8.0 * (rows[r + 1] - rows[r - 1]) - (rows[r + 2] - rows[r - 2])
                    mine = series_of(x, b, p.rg + r).astype(jnp.bfloat16)
                    along = jnp.dot(mine, inner_ref[...], preferred_element_type=jnp.float32)
                    out[b, r] = along - across

    outs = pltpu.VMEM((p.blocks, p.rg, p.nt, LANES), jnp.float32)
    return on_chip(body, [both, inner], outs, [])


def cross_spin_and(plan, base, wall, table, table_wall, owner, place, by_partner):
    p = plan
    _, outer = slope_taps(p)

    def prepare(place_ref, outer_ref, arrived, sides, slope, beside):
        chunk = place_ref[0] * p.blocks + place_ref[1]
        first = (chunk == 0).astype(jnp.int32)
        last = (chunk == p.chunks - 1).astype(jnp.int32)
        is_left = (lax.broadcasted_iota(jnp.int32, (p.nt, LANES), 1) & 3) < 2
        for m in range(p.ta):
            beside[m] = arrived[m][:, p.rg].astype(jnp.float32)

        def side_of(b):
            at = place_ref[1] ^ b if p.by_partner else b
            return jnp.concatenate([beside[place_ref[0] ^ t, at] for t in range(p.ta)], axis=0)

        for a in range(p.gx):
            for z in range(p.gz):
                before = a * p.gz + lax.rem(z + p.gz - first, p.gz)
                after = a * p.gz + lax.rem(z + last, p.gz)
                b = a * p.gz + z
                side = jnp.where(is_left, side_of(before), side_of(after))
                sides[b * p.nt : (b + 1) * p.nt, :] = side.astype(jnp.bfloat16)
        slope[...] = jnp.dot(sides[...], outer_ref[...], preferred_element_type=jnp.float32)

    scratch = [
        pltpu.VMEM((p.blocks * p.nt, LANES), jnp.bfloat16),
        pltpu.VMEM((p.blocks * p.nt, p.rg * LANES), jnp.float32),
        pltpu.VMEM((p.ta, p.blocks, p.tl, LANES), jnp.float32),
    ]
    jobs = [(wall, 0, table_wall), ([base], 0, table)]
    return cross(plan, jobs, owner, place, by_partner, (outer, prepare, scratch))


def cross(plan, jobs, owner, place, by_partner, spin=None):
    p = plan
    scaling = 8.0 / (3.0 * SEG * NSEG)
    pair = 2 if p.rg % 2 == 0 else 1
    width = pair * LANES
    inputs, where = [], []
    for series, start, table in jobs:
        if not any(x is series[0] for x in inputs):
            inputs.extend(series)
        if not any(x is table for x in inputs):
            inputs.append(table)
        first = next(i for i, x in enumerate(inputs) if x is series[0])
        where.append((first, len(series), start, next(i for i, x in enumerate(inputs) if x is table)))

    if spin is not None:
        outer, prepare, more_scratch = spin
        inputs.append(outer)

    def body(owner_ref, place_ref, *refs):
        outs = refs[len(inputs) : len(inputs) + n_outs]
        if by_partner:
            spec_0, spec_1, ref_0, ref_1 = refs[len(inputs) + n_outs :][:4]
            turns = ((spec_0, ref_0), (spec_1, ref_1))
        else:
            specs, ref_specs = refs[len(inputs) + n_outs :][:2]
            turns = tuple((specs.at[i], ref_specs.at[i]) for i in range(2))
        more = refs[len(refs) - 3 :]
        turn = 0
        for q, (first, count, start, table) in enumerate(where):
            whole = inputs[first].dtype == jnp.float32
            if whole:
                arrived = refs[where[0][0] : where[0][0] + where[0][1]]
                prepare(place_ref, refs[len(inputs) - 1], arrived, *more)
            for r in range(0, p.rg, pair):
                spec, ref_spec = turns[turn % 2]
                turn += 1
                for n in range(p.blocks):
                    rows = []
                    for i in range(pair):
                        at = start + r + i
                        if whole:
                            slope = more[1][n * p.nt : (n + 1) * p.nt, at * LANES : (at + 1) * LANES]
                            rows.append((refs[first][n, at] + slope) / 12.0)
                        elif count > 1:
                            x = [refs[first + m][n, at].astype(jnp.float32) for m in range(count)]
                            rows.append(jnp.concatenate(x, axis=0))
                        else:
                            rows.append(series_of(refs[first], n, at))
                    b = place_ref[1] ^ n if count > 1 and p.by_partner else n
                    spec[b] = jnp.dot(
                        refs[table][...],
                        jnp.concatenate(rows, axis=1).astype(jnp.bfloat16),
                        preferred_element_type=jnp.float32,
                    )
                for s in range(NSEG):
                    at = s * ROWS
                    ref_spec[at : at + ROWS, :] = spec[owner_ref[s], at : at + ROWS, :]
                for n in range(p.blocks):
                    b = place_ref[1] ^ n if by_partner else n
                    co = jnp.zeros((8, width), jnp.float32)
                    quad = jnp.zeros((8, width), jnp.float32)
                    for s in range(NSEG):
                        at = s * ROWS
                        rc, rs = ref_spec[at : at + 8, :], ref_spec[at + 8 : at + 16, :]
                        qc, qs = spec[b, at : at + 8, :], spec[b, at + 8 : at + 16, :]
                        co = co + (rc * qc + rs * qs)
                        quad = quad + (rc * qs - rs * qc)
                    both = (jnp.concatenate([co, quad], axis=0) * scaling).astype(jnp.bfloat16)
                    for i in range(pair):
                        mine = both[:, i * LANES : (i + 1) * LANES]
                        if by_partner:
                            outs[n][q, r + i] = mine
                        else:
                            outs[0][n, q, r + i] = mine

    shape = (len(jobs), p.rg, ROWS, LANES)
    if by_partner:
        outs = [pltpu.VMEM(shape, jnp.bfloat16) for _ in range(p.blocks)]
    else:
        outs = [pltpu.VMEM((p.blocks,) + shape, jnp.bfloat16)]
    n_outs = len(outs)
    spec_shape, ref_shape = (p.blocks, NSEG * ROWS, width), (NSEG * ROWS, width)
    if by_partner:
        scratch = [pltpu.VMEM(x, jnp.float32) for x in (spec_shape, spec_shape, ref_shape, ref_shape)]
    else:
        scratch = [pltpu.VMEM((2,) + x, jnp.float32) for x in (spec_shape, ref_shape)]
    scratch += more_scratch if spin is not None else []
    return on_chip(body, inputs, outs, scratch, (owner, place))


def assemble(plan, so_far, quantities, pieces, place):
    p = plan
    shape = (4, 2, F, p.xb, p.cs)
    if not p.fast:
        if len(pieces) > 1:
            x = jnp.stack(pieces)
            x = jnp.take(x, jnp.arange(p.blocks, dtype=jnp.int32) ^ place[1], axis=0)
        else:
            x = pieces[0]
        out = jnp.zeros(shape, jnp.float32) if so_far is None else so_far
        x = x.reshape(p.blocks, len(quantities), p.rg, 2, 8, p.groups, p.cc)[:, :, :, :, :F]
        x = x.transpose(1, 3, 4, 5, 2, 0, 6).reshape((-1,) + shape[1:]).astype(jnp.float32)
        for n, quantity in enumerate(quantities):
            out = out.at[quantity].set(x[n])
        return out

    def body(place_ref, *refs):
        xs, swap = refs[: len(pieces)], refs[len(pieces)]
        out, by_chunk, wide, held, sems = refs[-5:]
        copies, lhs = [], []
        tiles = p.cs // LANES
        for n in range(len(quantities)):
            for j in range(p.blocks):
                if len(pieces) > 1:
                    by_chunk[n, place_ref[1] ^ j] = xs[j][n].reshape(p.rg * ROWS, LANES)
                else:
                    by_chunk[n, j] = xs[0][j, n].reshape(p.rg * ROWS, LANES)
            for tile in range(tiles):
                columns = [by_chunk[n, tile * p.groups + i] for i in range(p.groups)]
                lhs.append(jnp.concatenate(columns, axis=1))
        swapped = jnp.dot(jnp.concatenate(lhs, axis=0), swap[...], preferred_element_type=jnp.float32)
        count = p.rg * ROWS
        for n, quantity in enumerate(quantities):
            for tile in range(tiles):
                at = (n * tiles + tile) * count
                for g in range(p.groups):
                    wide[n, tile, g] = swapped[at : at + count, g * LANES : (g + 1) * LANES]
            for part in range(2):
                for k in range(F):
                    for tile in range(tiles):
                        for g in range(p.groups):
                            block = wide[n, tile, g, pl.ds(part * 8 + k, p.rg, stride=ROWS), :]
                            rows = slice(g * p.rg, (g + 1) * p.rg)
                            held[n, part, k, rows, tile * LANES : (tile + 1) * LANES] = block
                copies.append(
                    pltpu.make_async_copy(held.at[n, part], out.at[quantity, part], sems.at[n, part])
                )
                copies[-1].start()
        for copy in copies:
            copy.wait()

    before = [] if so_far is None else [so_far]
    scratch = [
        pltpu.VMEM((len(quantities), p.blocks, p.rg * ROWS, LANES), jnp.bfloat16),
        pltpu.VMEM((len(quantities), p.cs // LANES, p.groups, p.rg * ROWS, LANES), jnp.float32),
        pltpu.VMEM((len(quantities),) + shape[1:], jnp.float32),
        pltpu.SemaphoreType.DMA((len(quantities), 2)),
    ]
    return on_chip(
        body,
        [*pieces, group_swap(p)] + before,
        jax.ShapeDtypeStruct(shape, jnp.float32),
        scratch,
        (place,),
        in_hbm=len(before),
        **({"input_output_aliases": {len(pieces) + 2: 0}} if before else {}),
    )


def shards(velocity, offsets, owner):
    plan = Plan(velocity)
    block_axes = ("gx", "gz")
    time = lax.axis_index("ta").astype(jnp.int32)
    place = jnp.stack([time, lax.axis_index(block_axes).astype(jnp.int32)])

    packed = pack_all(plan, velocity)
    both = packed.reshape((-1,) + packed.shape[2:])
    both = lax.all_to_all(both, block_axes + ("ta",), split_axis=0, concat_axis=0, tiled=True)
    both = both.reshape((plan.blocks, plan.ta) + both.shape[1:])

    def over_blocks(arrays):
        if len(arrays) == 1:
            return [lax.all_to_all(arrays[0], block_axes, split_axis=0, concat_axis=0, tiled=True)]
        traded = {n: trade(arrays[n], block_axes, n, plan.blocks) for n in range(1, plan.blocks)}
        return [arrays[0]] + [traded[n] for n in range(1, plan.blocks)]

    wall = pack_one(plan, velocity, 1, packed, place)
    wall = over_blocks(wall)
    wall = regroup(plan, wall)
    wall = [wall[0]] + [trade(wall[m], "ta", m, plan.ta) for m in range(1, plan.ta)]

    times = jnp.arange(plan.tl, dtype=jnp.int32)[None, :]
    turn = jnp.arange(plan.ta, dtype=jnp.int32)[:, None]
    table_wall = dft_rows(offsets, ((turn ^ time) * plan.tl + times).reshape(-1))
    table = dft_rows(offsets, (turn * plan.tl + times).reshape(-1))
    early = cross(plan, [([both], 0, table), ([both], plan.rg, table)], owner, place, False)
    early = over_blocks(early)
    base = inner_vorticity(plan, both)
    late = cross_spin_and(plan, base, wall, table, table_wall, owner, place, plan.by_partner)
    late = over_blocks(late)
    out = assemble(plan, None, (2, 0), early, place)
    return assemble(plan, out, (1, 3), late, place)


def solution(mesh):
    in_specs = (P(None, "ta", "gx", "gz"), P(), P())
    out_specs = P(None, None, None, "gx", ("gz", "ta"))

    return jax.shard_map(shards, mesh=mesh, in_specs=in_specs, out_specs=out_specs, check_vma=False)
```
